256 devices in a mesh: dp: 16 (over y, x_hi, core), expert: 16 (over z, x_lo).
Axes of the slice: x: 4 (x_hi: 2, x_lo: 2; x = x_hi * 2 + x_lo), y: 4, z: 8, core: 2. Of those that a mesh axis runs over, the one named last changes fastest.
Arguments:
- tokens: bfloat16 [32768, 2048], P(('dp', 'expert')), may hold values from -6 to 6
- routes: int32 [32768, 2], P(('dp', 'expert')), may hold values from 0 to 15, as said below
- grad_hidden: bfloat16 [32768, 2, 768], P(('dp', 'expert')), may hold values from -1.1953125 to 1.1953125
- w_gate: bfloat16 [16, 2048, 768], P('expert'), may hold values from -0.125 to 0.125
- w_up: bfloat16 [16, 2048, 768], P('expert'), may hold values from -0.125 to 0.125
Outputs:
- grad_tokens: bfloat16 [32768, 2048], P(('dp', 'expert'))
- grad_gate: float32 [16, 2048, 768], P('expert', 'dp')
- grad_up: float32 [16, 2048, 768], P('expert', 'dp')
The draws below stay inside these ranges and needn't reach their ends.
Inputs may be any that keep to these rules, and one draw needn't show every extreme that they name: `routes`: each row names 2 different experts. In each data group 2 experts are hot, the same for all rows of the group: in the rows of one device each hot expert of its group is named more often than every other expert and at most 46 times, every other expert at most 16 times. In the rows of every device some expert is named exactly 16 times; in the rows of some device a hot expert is named exactly 46 times. Every expert is hot in some data group. The indices of a group's two hot experts never differ by 8.
All inputs are finite; a program needn't handle non-finite values.
Results may differ from the reference program's by a relative error of at most 0.012.
Values may be sent and summed in bfloat16 or wider, within the bound.
No kernel may reach another device: no remote copies, remote signals or barrier semaphores. Data moves between devices by JAX's collectives and lax.ppermute only.
A program may use at most 128 MiB of HBM per device.

```python
import jax
import jax.numpy as jnp
from jax import lax

D = 2048
FF = 768
TOP = 2
TOK_DEV = 128
EXPERTS = 16
DATA_GROUPS = 16
ROW_TOKENS = 2048
TOKENS = 32768
COLD = 16
HMAX = 46
N_EXPERT = 16


def draw_routes(key, part):
    nblock = TOKENS // TOK_DEV
    pair_count = TOK_DEV * TOP
    cold_top = pair_count // EXPERTS
    cold_floor = cold_top - 2 - cold_top // 8
    subkeys = jax.random.split(key, 9)
    expert_ids = jnp.arange(EXPERTS, dtype=jnp.int32)
    block_ids = jnp.arange(nblock, dtype=jnp.int32)
    group_ids = block_ids // EXPERTS
    rotation = jax.random.randint(subkeys[0], (), 0, EXPERTS)
    first_hot = (rotation + group_ids) % EXPERTS
    group_offset = jax.random.randint(subkeys[1], (DATA_GROUPS,), 1, EXPERTS // 2)
    offset = group_offset[group_ids]
    second_hot = (first_hot + offset) % EXPERTS
    hot_one = expert_ids[None, :] == first_hot[:, None]
    hot_two = expert_ids[None, :] == second_hot[:, None]
    hot_flag = hot_one | hot_two
    load_table = jax.random.randint(subkeys[2], (nblock, EXPERTS), cold_floor, cold_top - 1)
    scores = jax.random.randint(subkeys[3], (nblock, EXPERTS), 0, 1 << 20) * EXPERTS + expert_ids[None, :]
    scores = jnp.where(hot_flag, -1, scores)
    forced = jnp.argmax(scores, axis=1).astype(jnp.int32)
    special = jax.random.randint(subkeys[4], (), 0, nblock)
    at_special = block_ids == special
    load_table = jnp.where(at_special[:, None], cold_floor, load_table)
    load_table = jnp.where(expert_ids[None, :] == forced[:, None], cold_top, load_table)
    load_table = jnp.where(hot_flag, 0, load_table)
    hot_total = pair_count - jnp.sum(load_table, axis=1)
    spread = jnp.minimum((hot_total - 2 * cold_top - 2) // 2, cold_top // 4)
    extra_load = jax.random.randint(subkeys[5], (nblock,), 0, spread + 1)
    extra_load = jnp.where(at_special, spread, extra_load)
    larger = (hot_total + 1) // 2 + extra_load
    smaller = hot_total - larger
    flipped = jax.random.randint(subkeys[6], (nblock,), 0, 2) == 1
    load_one = jnp.where(flipped, smaller, larger)
    load_two = jnp.where(flipped, larger, smaller)
    load_table = load_table + jnp.where(hot_one, load_one[:, None], 0) + jnp.where(hot_two, load_two[:, None], 0)

    def tickets(counts):
        return jnp.repeat(expert_ids, counts, total_repeat_length=pair_count)
    ticket_rows = jax.vmap(tickets)(load_table)
    pair_rows = jnp.stack([ticket_rows[:, :TOK_DEV], ticket_rows[:, TOK_DEV:]], axis=2)
    swapped = jax.random.randint(subkeys[7], (nblock, TOK_DEV, 1), 0, 2) == 1
    pair_rows = jnp.where(swapped, pair_rows[:, :, ::-1], pair_rows)

    def shuffle(block_key):
        return jax.random.permutation(block_key, TOK_DEV)
    token_order = jax.vmap(shuffle)(jax.random.split(subkeys[8], nblock))
    pair_rows = jnp.take_along_axis(pair_rows, token_order[:, :, None], axis=1)
    return pair_rows.reshape(TOKENS, TOP).astype(jnp.int32)


def shard_levels(key, shape, cuts, least, high):
    factor_of = 1.0
    for position, parts in cuts:
        draws = jax.random.uniform(jax.random.fold_in(jax.random.fold_in(key, 6), position), (parts,), jnp.float32, least / len(cuts), high / len(cuts))
        factor_of = factor_of * jnp.repeat(jnp.exp(draws), shape[position] // parts).reshape((-1,) + (1,) * (len(shape) - 1 - position))
    return factor_of


def normal_values(rng, extent, scale, limit, cuts=(), kind=jnp.bfloat16):
    result = jax.random.normal(rng, extent, jnp.float32) * scale
    if len(cuts) > 0:
        result = shard_levels(rng, extent, cuts, -0.22, 0.18) * result
    return jnp.clip(result, min=-limit, max=limit).astype(kind)


def setup_inputs(seed: int = 0) -> dict:
    streams_of = jax.random.split(jax.random.key(seed), 6)
    return {
        "tokens": normal_values(streams_of[0], (TOKENS, D), 1.0, 6.0, ((0, 256),)),
        "routes": draw_routes(jax.random.fold_in(streams_of[5], 71), 0),
        "grad_hidden": normal_values(streams_of[2], (TOKENS, TOP, FF), 0.2, 1.1953125, ((0, 256),)),
        "w_gate": normal_values(streams_of[3], (EXPERTS, D, FF), D ** -0.5, 0.125, ((0, 16),)),
        "w_up": normal_values(streams_of[4], (EXPERTS, D, FF), D ** -0.5, 0.125, ((0, 16),)),
    }


def expert_grads(rows_x, rows_dh, gate_w, up_w, spill_rows):
    gate_act = jnp.dot(rows_x, gate_w, preferred_element_type=jnp.float32)
    up_act = jnp.dot(rows_x, up_w, preferred_element_type=jnp.float32)
    gate_sig = jax.nn.sigmoid(gate_act)
    grad_wide = rows_dh.astype(jnp.float32)
    gate_delta = (grad_wide * up_act * gate_sig * (1.0 + gate_act * (1.0 - gate_sig))).astype(jnp.bfloat16)
    up_delta = (grad_wide * gate_act * gate_sig).astype(jnp.bfloat16)
    back_rows = lax.dot_general(gate_delta, gate_w, (((1,), (1,)), ((), ())), preferred_element_type=jnp.float32)
    back_rows = back_rows + lax.dot_general(up_delta, up_w, (((1,), (1,)), ((), ())), preferred_element_type=jnp.float32)
    zero_delta = jnp.zeros_like(gate_delta)
    gate_keep = jnp.where(spill_rows[:, None], zero_delta, gate_delta)
    gate_spill = jnp.where(spill_rows[:, None], gate_delta, zero_delta)
    up_keep = jnp.where(spill_rows[:, None], zero_delta, up_delta)
    up_spill = jnp.where(spill_rows[:, None], up_delta, zero_delta)
    dims = (((0,), (0,)), ((), ()))
    grads = tuple(lax.dot_general(rows_x, delta, dims, preferred_element_type=jnp.float32) for delta in (gate_keep, gate_spill, up_keep, up_spill))
    return back_rows.astype(jnp.bfloat16), grads


def reference(tokens, routes, grad_hidden, w_gate, w_up):
    row_pairs = ROW_TOKENS * TOP
    block_rows = 64
    slot_count = row_pairs + EXPERTS * block_rows
    block_count = slot_count // block_rows
    limit_rows = COLD + (HMAX - COLD + 1) // 2
    token_groups = tokens.reshape(DATA_GROUPS, ROW_TOKENS, D)
    route_groups = routes.reshape(DATA_GROUPS, row_pairs)
    grad_groups = grad_hidden.reshape(DATA_GROUPS, row_pairs, FF)
    expert_ids = jnp.arange(EXPERTS, dtype=jnp.int32)

    def one_group(totals, items):
        group_tokens, group_routes, group_grads = items
        device_routes = group_routes.reshape(N_EXPERT, TOK_DEV * TOP)
        member = (device_routes[:, :, None] == expert_ids[None, None, :]).astype(jnp.int32)
        ranked = jnp.sum(jnp.cumsum(member, axis=1) * member, axis=2) - 1
        spill_flag = (ranked >= limit_rows).reshape(row_pairs)
        padded_spill = jnp.concatenate([spill_flag, jnp.zeros((1,), bool)], axis=0)
        counts = jnp.sum((group_routes[:, None] == expert_ids[None, :]).astype(jnp.int32), axis=0)
        padded = (counts + block_rows - 1) // block_rows * block_rows
        offsets = jnp.cumsum(padded) - padded
        starts = jnp.cumsum(counts) - counts
        ordering = jnp.argsort(group_routes, stable=True).astype(jnp.int32)
        sorted_ids = group_routes[ordering]
        slot_of = offsets[sorted_ids] + jnp.arange(row_pairs, dtype=jnp.int32) - starts[sorted_ids]
        slot_table = jnp.full((slot_count,), row_pairs, jnp.int32).at[slot_of].set(ordering)
        end_of = offsets + padded
        block_start = jnp.arange(block_count, dtype=jnp.int32) * block_rows
        block_owner = jnp.minimum(jnp.sum((block_start[:, None] >= end_of[None, :]).astype(jnp.int32), axis=1), EXPERTS - 1)
        padded_tokens = jnp.concatenate([group_tokens, jnp.zeros((1, D), group_tokens.dtype)], axis=0)
        padded_grads = jnp.concatenate([group_grads, jnp.zeros((1, FF), group_grads.dtype)], axis=0)

        def one_block(accums, block_index):
            picked = lax.dynamic_slice_in_dim(slot_table, block_index * block_rows, block_rows)
            tok_index = jnp.where(picked < row_pairs, picked // TOP, ROW_TOKENS).astype(jnp.int32)
            rows_x = padded_tokens[tok_index]
            rows_dh = padded_grads[picked]
            spill_rows = padded_spill[picked]
            expert_now = block_owner[block_index]
            back_rows, grads = expert_grads(rows_x, rows_dh, w_gate[expert_now], w_up[expert_now], spill_rows)
            new_accums = tuple(acc.at[expert_now].add(part) for acc, part in zip(accums, grads))
            return new_accums, back_rows

        zero_grads = jnp.zeros((EXPERTS, D, FF), jnp.float32)
        accums, pair_backs = lax.scan(one_block, (zero_grads, zero_grads, zero_grads, zero_grads), jnp.arange(block_count, dtype=jnp.int32))
        pair_back = jnp.zeros((row_pairs + 1, D), jnp.bfloat16).at[slot_table].set(pair_backs.reshape(slot_count, D))[:row_pairs]
        rounded = [lax.optimization_barrier(acc.astype(jnp.bfloat16)).astype(jnp.float32) for acc in accums]
        return (totals[0] + rounded[0] + rounded[1], totals[1] + rounded[2] + rounded[3]), pair_back

    zero_grads = jnp.zeros((EXPERTS, D, FF), jnp.float32)
    grads, pair_backs = lax.scan(one_group, (zero_grads, zero_grads), (token_groups, route_groups, grad_groups))
    pair_backs = lax.optimization_barrier(pair_backs)
    grad_tokens = jnp.sum(pair_backs.reshape(TOKENS, TOP, D).astype(jnp.float32), axis=1).astype(jnp.bfloat16)
    return grad_tokens, grads[0], grads[1]
```

```python
import functools

import jax
import jax.numpy as jnp
import numpy as np
from jax import lax
from jax.experimental import pallas as pl
from jax.experimental.pallas import tpu as pltpu
from jax.sharding import PartitionSpec as P

D = 2048
FF = 768
EXPERTS = 16
CAP = 48
ROWS = EXPERTS * CAP
BLOCK = 128
FF_BLOCK = 256
MIB = 1 << 20


def pack_kernel(routes_ref, tokens_ref, grads_ref, sel_ref, out_ref):
    pairs = routes_ref.shape[1]
    toks = tokens_ref.shape[0]
    rows = out_ref.shape[0]
    routes = routes_ref[...]
    member = (routes == lax.broadcasted_iota(jnp.int32, (EXPERTS, pairs), 0)).astype(jnp.bfloat16)
    earlier = (
        lax.broadcasted_iota(jnp.int32, (pairs, pairs), 0)
        < lax.broadcasted_iota(jnp.int32, (pairs, pairs), 1)
    ).astype(jnp.bfloat16)
    before = jnp.dot(member, earlier, preferred_element_type=jnp.float32)
    rank = jnp.sum(member.astype(jnp.float32) * before, axis=0, keepdims=True).astype(jnp.int32)
    slot = routes * CAP + rank
    first = pl.program_id(0) * rows
    pick = (slot == first + lax.broadcasted_iota(jnp.int32, (rows, pairs), 0)).astype(jnp.bfloat16)
    to_token = (
        lax.broadcasted_iota(jnp.int32, (pairs, toks), 0) // 2
        == lax.broadcasted_iota(jnp.int32, (pairs, toks), 1)
    ).astype(jnp.bfloat16)
    pick_token = jnp.dot(pick, to_token, preferred_element_type=jnp.float32).astype(jnp.bfloat16)
    sel_ref[...] = pick_token
    out_ref[:, :D] = jnp.dot(
        pick_token, tokens_ref[...], preferred_element_type=jnp.float32
    ).astype(jnp.bfloat16)
    out_ref[:, D:] = jnp.dot(pick, grads_ref[...], preferred_element_type=jnp.float32).astype(
        jnp.bfloat16
    )


def pack(routes, tokens, grads):
    steps = 4
    toks, pairs = tokens.shape[0], grads.shape[0]
    return pl.pallas_call(
        pack_kernel,
        grid=(steps,),
        in_specs=[
            pl.BlockSpec((1, pairs), lambda i: (0, 0)),
            pl.BlockSpec((toks, D), lambda i: (0, 0)),
            pl.BlockSpec((pairs, FF), lambda i: (0, 0)),
        ],
        out_specs=[
            pl.BlockSpec((ROWS // steps, toks), lambda i: (i, 0)),
            pl.BlockSpec((ROWS // steps, D + FF), lambda i: (i, 0)),
        ],
        out_shape=[
            jax.ShapeDtypeStruct((ROWS, toks), jnp.bfloat16),
            jax.ShapeDtypeStruct((ROWS, D + FF), jnp.bfloat16),
        ],
        compiler_params=pltpu.CompilerParams(vmem_limit_bytes=32 * MIB),
        cost_estimate=pl.CostEstimate(flops=10**9, bytes_accessed=6 * MIB, transcendentals=0),
        name="pack",
    )(routes, tokens, grads)


def expert_kernel(x_ref, dh_ref, wg_ref, wu_ref, delta_g_ref, delta_u_ref, back_ref, acc_ref):
    j = pl.program_id(0)
    x = x_ref[...]
    wg = wg_ref[0]
    wu = wu_ref[0]
    gate = jnp.dot(x, wg, preferred_element_type=jnp.float32)
    up = jnp.dot(x, wu, preferred_element_type=jnp.float32)
    sig = jax.nn.sigmoid(gate)
    wide = dh_ref[...].astype(jnp.float32)
    delta_g = (wide * up * sig * (1.0 + gate * (1.0 - sig))).astype(jnp.bfloat16)
    delta_u = (wide * gate * sig).astype(jnp.bfloat16)
    delta_g_ref[...] = delta_g
    delta_u_ref[...] = delta_u
    dims = (((1,), (1,)), ((), ()))
    part = lax.dot_general(
        delta_g, wg, dims, preferred_element_type=jnp.float32
    ) + lax.dot_general(delta_u, wu, dims, preferred_element_type=jnp.float32)
    last = pl.num_programs(0) - 1

    @pl.when(j == 0)
    def _():
        acc_ref[...] = part

    @pl.when(jnp.logical_and(j > 0, j < last))
    def _():
        acc_ref[...] += part

    @pl.when(j == last)
    def _():
        back_ref[...] = (acc_ref[...] + part).astype(jnp.bfloat16)


def expert(got, w_gate, w_up):
    steps = FF // FF_BLOCK
    off = D // FF_BLOCK
    return pl.pallas_call(
        expert_kernel,
        grid=(steps,),
        in_specs=[
            pl.BlockSpec((ROWS, D), lambda j: (0, 0)),
            pl.BlockSpec((ROWS, FF_BLOCK), lambda j: (0, off + j)),
            pl.BlockSpec((1, D, FF_BLOCK), lambda j: (0, 0, j)),
            pl.BlockSpec((1, D, FF_BLOCK), lambda j: (0, 0, j)),
        ],
        out_specs=[
            pl.BlockSpec((ROWS, FF_BLOCK), lambda j: (0, j)),
            pl.BlockSpec((ROWS, FF_BLOCK), lambda j: (0, j)),
            pl.BlockSpec((ROWS, D), lambda j: (0, 0)),
        ],
        out_shape=[
            jax.ShapeDtypeStruct((ROWS, FF), jnp.bfloat16),
            jax.ShapeDtypeStruct((ROWS, FF), jnp.bfloat16),
            jax.ShapeDtypeStruct((ROWS, D), jnp.bfloat16),
        ],
        scratch_shapes=[pltpu.VMEM((ROWS, D), jnp.float32)],
        compiler_params=pltpu.CompilerParams(vmem_limit_bytes=48 * MIB),
        cost_estimate=pl.CostEstimate(
            flops=8 * ROWS * D * FF, bytes_accessed=17 * MIB, transcendentals=ROWS * FF
        ),
        name="expert",
    )(got, got, w_gate, w_up)


def weight_part(x_ref, dg_ref, du_ref):
    dims = (((0,), (0,)), ((), ()))
    x = x_ref[...]
    return (
        lax.dot_general(x, dg_ref[...], dims, preferred_element_type=jnp.float32),
        lax.dot_general(x, du_ref[...], dims, preferred_element_type=jnp.float32),
    )


def weight_send_kernel(block_ref, x_ref, dg_ref, du_ref, out_ref):
    gate, up = weight_part(x_ref, dg_ref, du_ref)
    out_ref[:, :FF] = gate.astype(jnp.bfloat16)
    out_ref[:, FF:] = up.astype(jnp.bfloat16)


def weight_specs():
    return [
        pl.BlockSpec((ROWS, BLOCK), lambda i, b: (0, b[i])),
        pl.BlockSpec((ROWS, FF), lambda i, b: (0, 0)),
        pl.BlockSpec((ROWS, FF), lambda i, b: (0, 0)),
    ]


def weight_send(blocks, got, delta_g, delta_u):
    count = blocks.shape[0]
    return pl.pallas_call(
        weight_send_kernel,
        grid_spec=pltpu.PrefetchScalarGridSpec(
            num_scalar_prefetch=1,
            grid=(count,),
            in_specs=weight_specs(),
            out_specs=pl.BlockSpec((BLOCK, 2 * FF), lambda i, b: (i, 0)),
        ),
        out_shape=jax.ShapeDtypeStruct((count * BLOCK, 2 * FF), jnp.bfloat16),
        compiler_params=pltpu.CompilerParams(vmem_limit_bytes=32 * MIB),
        cost_estimate=pl.CostEstimate(
            flops=4 * ROWS * count * BLOCK * FF, bytes_accessed=8 * MIB, transcendentals=0
        ),
        name="weight_send",
    )(blocks, got, delta_g, delta_u)


def weight_keep_kernel(block_ref, x_ref, dg_ref, du_ref, came_ref, own_ref, *out_refs):
    i = pl.program_id(0)
    gate, up = weight_part(x_ref, dg_ref, du_ref)
    gate = gate + came_ref[:, :FF].astype(jnp.float32)
    up = up + came_ref[:, FF:].astype(jnp.float32)

    @pl.when(i == 0)
    def _():
        own_ref[:, :FF] = gate
        own_ref[:, FF:] = up

    for k, out_ref in enumerate(out_refs):

        @pl.when(i == k + 1)
        def _(out_ref=out_ref):
            out_ref[:, :FF] = gate.astype(jnp.bfloat16)
            out_ref[:, FF:] = up.astype(jnp.bfloat16)


def weight_keep(blocks, got, delta_g, delta_u, came):
    count = blocks.shape[0]
    whole = pl.BlockSpec((BLOCK, 2 * FF), lambda i, b: (0, 0))
    return pl.pallas_call(
        weight_keep_kernel,
        grid_spec=pltpu.PrefetchScalarGridSpec(
            num_scalar_prefetch=1,
            grid=(count,),
            in_specs=weight_specs() + [pl.BlockSpec((BLOCK, 2 * FF), lambda i, b: (i, 0))],
            out_specs=[whole] * count,
        ),
        out_shape=[jax.ShapeDtypeStruct((BLOCK, 2 * FF), jnp.float32)]
        + [jax.ShapeDtypeStruct((BLOCK, 2 * FF), jnp.bfloat16)] * (count - 1),
        compiler_params=pltpu.CompilerParams(vmem_limit_bytes=40 * MIB),
        cost_estimate=pl.CostEstimate(
            flops=4 * ROWS * count * BLOCK * FF, bytes_accessed=11 * MIB, transcendentals=0
        ),
        name="weight_keep",
    )(blocks, got, delta_g, delta_u, came)


def place(index):
    return index // 4, index // 2 % 2, index % 2


def partner(index, step):
    y, x, core = place(index)
    return (y + step // 2) % 4 * 4 + (x + step % 2) % 2 * 2 + core


def per_device(tokens, routes, grad_hidden, w_gate, w_up):
    toks, per_token = routes.shape
    pairs = toks * per_token
    groups = lax.axis_size("dp")
    steps = groups // 2
    sel, send = pack(
        routes.reshape(1, pairs), tokens, grad_hidden.reshape(pairs, grad_hidden.shape[2])
    )
    got = lax.all_to_all(send, "expert", split_axis=0, concat_axis=0, tiled=True)
    delta_g, delta_u, back = expert(got, w_gate, w_up)
    returned = lax.all_to_all(back, "expert", split_axis=0, concat_axis=0, tiled=True)

    keep_table = np.array([[partner(i, s) for s in range(steps)] for i in range(groups)], np.int32)
    me = lax.axis_index("dp")
    keep_blocks = jnp.asarray(keep_table)[me]
    other_half = weight_send(keep_blocks ^ 1, got, delta_g, delta_u)
    came = lax.ppermute(other_half, "dp", [(i, i ^ 1) for i in range(groups)])
    own, *parts = weight_keep(keep_blocks, got, delta_g, delta_u, came)
    total = own
    for s, part in enumerate(parts, 1):
        came = lax.ppermute(part, "dp", [(i, partner(i, s)) for i in range(groups)])
        total = total + came.astype(jnp.float32)
    grad_tokens = lax.dot_general(
        sel, returned, (((0,), (0,)), ((), ())), preferred_element_type=jnp.float32
    ).astype(jnp.bfloat16)
    return grad_tokens, total[None, :, :FF], total[None, :, FF:]


def solution(mesh):
    placed = (
        P(("dp", "expert"), None),
        P(("dp", "expert"), None),
        P(("dp", "expert"), None, None),
        P("expert", None, None),
        P("expert", None, None),
    )
    return jax.shard_map(
        per_device,
        mesh=mesh,
        in_specs=placed,
        out_specs=(P(("dp", "expert"), None), P("expert", "dp", None), P("expert", "dp", None)),
        check_vma=False,
    )
```

```python
import functools

import jax
import jax.numpy as jnp
import numpy as np
from jax import lax
from jax.experimental import pallas as pl
from jax.experimental.pallas import tpu as pltpu
from jax.sharding import PartitionSpec as P

D = 2048
FF = 768
EXPERTS = 16
COLD = 16
SPILL = 32
CAP = COLD + SPILL
ROWS = EXPERTS * CAP
DIRECT = EXPERTS * COLD
OVER = EXPERTS * SPILL
WIDTH = D + FF
OFFSETS = (0, -1, 1, -2, 2, -3, 3, 4)
PIECES = ((0, 3), (3, 5), (5, 7), (7, 8))
BLOCK = 128
FF_BLOCK = 256
MIB = 1 << 20


def pack_kernel(me_ref, routes_ref, tokens_ref, grads_ref, choice_ref, sel_ref, out_ref, over_ref):
    pairs = routes_ref.shape[1]
    toks = tokens_ref.shape[0]
    me = me_ref[0]
    routes = routes_ref[...]
    member = (routes == lax.broadcasted_iota(jnp.int32, (EXPERTS, pairs), 0)).astype(jnp.float32)
    member_low = member.astype(jnp.bfloat16)
    earlier = (
        lax.broadcasted_iota(jnp.int32, (pairs, pairs), 0)
        < lax.broadcasted_iota(jnp.int32, (pairs, pairs), 1)
    ).astype(jnp.bfloat16)
    before = jnp.dot(member_low, earlier, preferred_element_type=jnp.float32)
    rank = jnp.sum(member * before, axis=0, keepdims=True).astype(jnp.int32)

    count_col = jnp.sum(member, axis=1, keepdims=True)
    count_row = lax.dot_general(
        jnp.ones((8, pairs), jnp.bfloat16),
        member_low,
        (((1,), (1,)), ((), ())),
        preferred_element_type=jnp.float32,
    )[:1]
    down = lax.broadcasted_iota(jnp.int32, (EXPERTS, EXPERTS), 0)
    across = lax.broadcasted_iota(jnp.int32, (EXPERTS, EXPERTS), 1)
    above_col = jnp.sum((count_row > count_col).astype(jnp.float32), axis=1, keepdims=True)
    above_row = jnp.sum((count_col > count_row).astype(jnp.float32), axis=0, keepdims=True)
    hot_col = (above_col < 1.5).astype(jnp.float32)
    hot_row = (above_row < 1.5).astype(jnp.float32)
    which_col = jnp.sum(hot_row * (across < down).astype(jnp.float32), axis=1, keepdims=True)
    which_row = jnp.sum(hot_col * (down < across).astype(jnp.float32), axis=0, keepdims=True)
    which = jnp.sum(member * which_col, axis=0, keepdims=True).astype(jnp.int32)

    lane16 = lax.broadcasted_iota(jnp.int32, (1, EXPERTS), 1)
    mine = (lane16 == me).astype(jnp.float32)
    beside = (lane16 == me + 1 - 2 * (me % 2)).astype(jnp.float32)
    hot_me = jnp.sum(mine * hot_row, axis=1, keepdims=True)
    slot_me = jnp.sum(mine * hot_row * which_row, axis=1, keepdims=True)
    slot_beside = jnp.sum(beside * hot_row * which_row, axis=1, keepdims=True)
    lane = lax.broadcasted_iota(jnp.int32, (1, 128), 1)
    choice_ref[...] = jnp.where(
        lane == 0,
        slot_me.astype(jnp.int32),
        jnp.where(
            lane == 1,
            hot_me.astype(jnp.int32),
            jnp.where(lane == 2, slot_beside.astype(jnp.int32), me),
        ),
    )

    to_token = (
        lax.broadcasted_iota(jnp.int32, (pairs, toks), 0) // 2
        == lax.broadcasted_iota(jnp.int32, (pairs, toks), 1)
    ).astype(jnp.bfloat16)

    def picked(slot, rows):
        pick = (slot == lax.broadcasted_iota(jnp.int32, (rows, pairs), 0)).astype(jnp.bfloat16)
        tok = jnp.dot(pick, to_token, preferred_element_type=jnp.float32).astype(jnp.bfloat16)
        return pick, tok

    def fill(ref, slot):
        pick, tok = picked(slot, ref.shape[0])
        ref[:, :D] = jnp.dot(tok, tokens_ref[...], preferred_element_type=jnp.float32).astype(
            jnp.bfloat16
        )
        ref[:, D:] = jnp.dot(pick, grads_ref[...], preferred_element_type=jnp.float32).astype(
            jnp.bfloat16
        )

    fill(over_ref, jnp.where(rank >= COLD, which * SPILL + rank - COLD, -1))
    fill(out_ref, jnp.where(rank < COLD, routes * COLD + rank, -1))
    sel_ref[...] = picked(routes * CAP + rank, ROWS)[1]


def pack(me, routes, tokens, grads):
    toks, pairs = tokens.shape[0], grads.shape[0]
    vmem = pl.BlockSpec(memory_space=pltpu.VMEM)
    return pl.pallas_call(
        pack_kernel,
        in_specs=[pl.BlockSpec(memory_space=pltpu.SMEM), vmem, vmem, vmem],
        out_specs=[vmem] * 4,
        out_shape=[
            jax.ShapeDtypeStruct((1, 128), jnp.int32),
            jax.ShapeDtypeStruct((ROWS, toks), jnp.bfloat16),
            jax.ShapeDtypeStruct((DIRECT, WIDTH), jnp.bfloat16),
            jax.ShapeDtypeStruct((2 * SPILL, WIDTH), jnp.bfloat16),
        ],
        compiler_params=pltpu.CompilerParams(vmem_limit_bytes=12 * MIB),
        cost_estimate=pl.CostEstimate(flops=10**9, bytes_accessed=4 * MIB, transcendentals=0),
        name="pack",
    )(me, routes, tokens, grads)


def choose_kernel(choice_ref, *refs):
    for k, ref in enumerate(refs[:-1]):
        refs[-1][k * SPILL : (k + 1) * SPILL, :] = ref[...]


def choose(choice, blocks):
    count = len(blocks)
    return pl.pallas_call(
        choose_kernel,
        grid_spec=pltpu.PrefetchScalarGridSpec(
            num_scalar_prefetch=1,
            grid=(1,),
            in_specs=[pl.BlockSpec((SPILL, WIDTH), lambda i, c: (c[2], 0))] * count,
            out_specs=pl.BlockSpec((count * SPILL, WIDTH), lambda i, c: (0, 0)),
        ),
        out_shape=jax.ShapeDtypeStruct((count * SPILL, WIDTH), jnp.bfloat16),
        compiler_params=pltpu.CompilerParams(vmem_limit_bytes=4 * MIB),
        cost_estimate=pl.CostEstimate(
            flops=0, bytes_accessed=4 * count * SPILL * WIDTH, transcendentals=0
        ),
        name="choose",
    )(choice, *blocks)


def deltas(x, dh, wg, wu):
    gate = jnp.dot(x, wg, preferred_element_type=jnp.float32)
    up = jnp.dot(x, wu, preferred_element_type=jnp.float32)
    sig = jax.nn.sigmoid(gate)
    wide = dh.astype(jnp.float32)
    delta_g = (wide * up * sig * (1.0 + gate * (1.0 - sig))).astype(jnp.bfloat16)
    delta_u = (wide * gate * sig).astype(jnp.bfloat16)
    dims = (((1,), (1,)), ((), ()))
    part = lax.dot_general(
        delta_g, wg, dims, preferred_element_type=jnp.float32
    ) + lax.dot_general(delta_u, wu, dims, preferred_element_type=jnp.float32)
    return delta_g, delta_u, part


def over_kernel(choice_ref, *refs):
    column = refs[:8]
    pieces = refs[8 : 8 + len(PIECES)]
    wg_ref, wu_ref, x_ref, delta_g_ref, delta_u_ref, back_ref, acc_ref, dh_ref = refs[
        8 + len(PIECES) :
    ]
    j = pl.program_id(0)
    last = pl.num_programs(0) - 1
    hot = choice_ref[1] == 1

    @pl.when(j == 0)
    def _():
        back_ref[...] = jnp.zeros_like(back_ref)
        at = 0
        for ref in (*column, *pieces):
            rows = ref.shape[0]
            x_ref[at : at + rows, :] = ref[:, :D]
            for k in range(FF // FF_BLOCK):
                dh_ref[k, at : at + rows, :] = ref[
                    :, D + k * FF_BLOCK : D + (k + 1) * FF_BLOCK
                ]
            at += rows

    @pl.when(jnp.logical_not(hot))
    def _():
        delta_g_ref[...] = jnp.zeros_like(delta_g_ref)
        delta_u_ref[...] = jnp.zeros_like(delta_u_ref)

    @pl.when(hot)
    def _():
        delta_g, delta_u, part = deltas(x_ref[...], dh_ref[j], wg_ref[0], wu_ref[0])
        delta_g_ref[...] = delta_g
        delta_u_ref[...] = delta_u

        @pl.when(j == 0)
        def _():
            acc_ref[...] = part

        @pl.when(jnp.logical_and(j > 0, j < last))
        def _():
            acc_ref[...] += part

        @pl.when(j == last)
        def _():
            acc_ref[...] += part
            me = choice_ref[3]
            for k in range(2 * len(OFFSETS)):
                source = (me + 2 * OFFSETS[k % 8] + EXPERTS) % EXPERTS
                if k >= 8:
                    source = source + 1 - 2 * (source % 2)
                row = pl.multiple_of(source * CAP + COLD, COLD)
                back_ref[pl.ds(row, SPILL), :] = acc_ref[
                    k * SPILL : (k + 1) * SPILL, :
                ].astype(jnp.bfloat16)


def over(choice, column, pieces, w_gate, w_up):
    steps = FF // FF_BLOCK
    return pl.pallas_call(
        over_kernel,
        grid_spec=pltpu.PrefetchScalarGridSpec(
            num_scalar_prefetch=1,
            grid=(steps,),
            in_specs=[pl.BlockSpec((SPILL, WIDTH), lambda j, c: (c[0], 0))] * len(column)
            + [pl.BlockSpec(p.shape, lambda j, c: (0, 0)) for p in pieces]
            + [pl.BlockSpec((1, D, FF_BLOCK), lambda j, c: (0, 0, j))] * 2,
            out_specs=[
                pl.BlockSpec((OVER, D), lambda j, c: (0, 0)),
                pl.BlockSpec((OVER, FF_BLOCK), lambda j, c: (0, j)),
                pl.BlockSpec((OVER, FF_BLOCK), lambda j, c: (0, j)),
                pl.BlockSpec((ROWS, D), lambda j, c: (0, 0)),
            ],
            scratch_shapes=[
                pltpu.VMEM((OVER, D), jnp.float32),
                pltpu.VMEM((steps, OVER, FF_BLOCK), jnp.bfloat16),
            ],
        ),
        out_shape=[
            jax.ShapeDtypeStruct((OVER, D), jnp.bfloat16),
            jax.ShapeDtypeStruct((OVER, FF), jnp.bfloat16),
            jax.ShapeDtypeStruct((OVER, FF), jnp.bfloat16),
            pltpu.HBM((ROWS, D), jnp.bfloat16),
        ],
        compiler_params=pltpu.CompilerParams(vmem_limit_bytes=34 * MIB),
        cost_estimate=pl.CostEstimate(
            flops=8 * OVER * D * FF, bytes_accessed=17 * MIB, transcendentals=OVER * FF
        ),
        name="over",
    )(choice, *column, *pieces, w_gate, w_up)


def direct_kernel(
    x_ref, dh_ref, wg_ref, wu_ref, old_ref, delta_g_ref, delta_u_ref, back_ref, acc_ref, low_ref, sems
):
    j = pl.program_id(0)
    delta_g, delta_u, part = deltas(x_ref[...], dh_ref[...], wg_ref[0], wu_ref[0])
    delta_g_ref[...] = delta_g
    delta_u_ref[...] = delta_u
    last = pl.num_programs(0) - 1

    @pl.when(j == 0)
    def _():
        acc_ref[...] = part

    @pl.when(jnp.logical_and(j > 0, j < last))
    def _():
        acc_ref[...] += part

    @pl.when(j == last)
    def _():
        low_ref[...] = (acc_ref[...] + part).astype(jnp.bfloat16)
        copies = [
            pltpu.make_async_copy(
                low_ref.at[pl.ds(e * COLD, COLD), :],
                back_ref.at[pl.ds(e * CAP, COLD), :],
                sems.at[e],
            )
            for e in range(EXPERTS)
        ]
        for copy in copies:
            copy.start()
        for copy in copies:
            copy.wait()


def direct(got, w_gate, w_up, back):
    steps = FF // FF_BLOCK
    off = D // FF_BLOCK
    return pl.pallas_call(
        direct_kernel,
        grid=(steps,),
        in_specs=[
            pl.BlockSpec((DIRECT, D), lambda j: (0, 0)),
            pl.BlockSpec((DIRECT, FF_BLOCK), lambda j: (0, off + j)),
            pl.BlockSpec((1, D, FF_BLOCK), lambda j: (0, 0, j)),
            pl.BlockSpec((1, D, FF_BLOCK), lambda j: (0, 0, j)),
            pl.BlockSpec(memory_space=pltpu.HBM),
        ],
        out_specs=[
            pl.BlockSpec((DIRECT, FF_BLOCK), lambda j: (0, j)),
            pl.BlockSpec((DIRECT, FF_BLOCK), lambda j: (0, j)),
            pl.BlockSpec(memory_space=pltpu.HBM),
        ],
        out_shape=[
            jax.ShapeDtypeStruct((DIRECT, FF), jnp.bfloat16),
            jax.ShapeDtypeStruct((DIRECT, FF), jnp.bfloat16),
            pltpu.HBM((ROWS, D), jnp.bfloat16),
        ],
        scratch_shapes=[
            pltpu.VMEM((DIRECT, D), jnp.float32),
            pltpu.VMEM((DIRECT, D), jnp.bfloat16),
            pltpu.SemaphoreType.DMA((EXPERTS,)),
        ],
        input_output_aliases={4: 2},
        compiler_params=pltpu.CompilerParams(vmem_limit_bytes=20 * MIB),
        cost_estimate=pl.CostEstimate(
            flops=8 * DIRECT * D * FF, bytes_accessed=10 * MIB, transcendentals=DIRECT * FF
        ),
        name="direct",
    )(got, got, w_gate, w_up, pltpu.with_memory_space_constraint(back, pltpu.HBM))


def weight_part(x_ref, dg_ref, du_ref, over_x_ref, over_dg_ref, over_du_ref):
    dims = (((0,), (0,)), ((), ()))
    x = x_ref[...]
    over_x = over_x_ref[...]

    def both(d_ref, over_d_ref):
        return lax.dot_general(
            x, d_ref[...], dims, preferred_element_type=jnp.float32
        ) + lax.dot_general(over_x, over_d_ref[...], dims, preferred_element_type=jnp.float32)

    return both(dg_ref, over_dg_ref), both(du_ref, over_du_ref)


def weight_send_kernel(block_ref, *refs):
    gate, up = weight_part(*refs[:6])
    out_ref = refs[6]
    out_ref[:, :FF] = gate.astype(jnp.bfloat16)
    out_ref[:, FF:] = up.astype(jnp.bfloat16)


def weight_specs():
    return [
        pl.BlockSpec((DIRECT, BLOCK), lambda i, b: (0, b[i])),
        pl.BlockSpec((DIRECT, FF), lambda i, b: (0, 0)),
        pl.BlockSpec((DIRECT, FF), lambda i, b: (0, 0)),
        pl.BlockSpec((OVER, BLOCK), lambda i, b: (0, b[i])),
        pl.BlockSpec((OVER, FF), lambda i, b: (0, 0)),
        pl.BlockSpec((OVER, FF), lambda i, b: (0, 0)),
    ]


def weight_send(blocks, rows):
    count = blocks.shape[0]
    return pl.pallas_call(
        weight_send_kernel,
        grid_spec=pltpu.PrefetchScalarGridSpec(
            num_scalar_prefetch=1,
            grid=(count,),
            in_specs=weight_specs(),
            out_specs=pl.BlockSpec((BLOCK, 2 * FF), lambda i, b: (i, 0)),
        ),
        out_shape=jax.ShapeDtypeStruct((count * BLOCK, 2 * FF), jnp.bfloat16),
        compiler_params=pltpu.CompilerParams(vmem_limit_bytes=18 * MIB),
        cost_estimate=pl.CostEstimate(
            flops=4 * ROWS * count * BLOCK * FF, bytes_accessed=8 * MIB, transcendentals=0
        ),
        name="weight_send",
    )(blocks, *rows)


def weight_keep_kernel(block_ref, *refs):
    i = pl.program_id(0)
    came_ref, own_ref, *out_refs = refs[6:]
    gate, up = weight_part(*refs[:6])
    gate = gate + came_ref[:, :FF].astype(jnp.float32)
    up = up + came_ref[:, FF:].astype(jnp.float32)

    @pl.when(i == 0)
    def _():
        own_ref[:, :FF] = gate
        own_ref[:, FF:] = up

    for k, out_ref in enumerate(out_refs):

        @pl.when(i == k + 1)
        def _(out_ref=out_ref):
            out_ref[:, :FF] = gate.astype(jnp.bfloat16)
            out_ref[:, FF:] = up.astype(jnp.bfloat16)


def weight_keep(blocks, rows, came):
    count = blocks.shape[0]
    whole = pl.BlockSpec((BLOCK, 2 * FF), lambda i, b: (0, 0))
    return pl.pallas_call(
        weight_keep_kernel,
        grid_spec=pltpu.PrefetchScalarGridSpec(
            num_scalar_prefetch=1,
            grid=(count,),
            in_specs=weight_specs() + [pl.BlockSpec((BLOCK, 2 * FF), lambda i, b: (i, 0))],
            out_specs=[whole] * count,
        ),
        out_shape=[jax.ShapeDtypeStruct((BLOCK, 2 * FF), jnp.float32)]
        + [jax.ShapeDtypeStruct((BLOCK, 2 * FF), jnp.bfloat16)] * (count - 1),
        compiler_params=pltpu.CompilerParams(vmem_limit_bytes=24 * MIB),
        cost_estimate=pl.CostEstimate(
            flops=4 * ROWS * count * BLOCK * FF, bytes_accessed=11 * MIB, transcendentals=0
        ),
        name="weight_keep",
    )(blocks, *rows, came)


def place(index):
    return index // 4, index // 2 % 2, index % 2


def partner(index, step):
    y, x, core = place(index)
    return (y + step // 2) % 4 * 4 + (x + step % 2) % 2 * 2 + core


def per_device(tokens, routes, grad_hidden, w_gate, w_up):
    toks, per_token = routes.shape
    pairs = toks * per_token
    groups = lax.axis_size("dp")
    steps = groups // 2
    expert_at = lax.axis_index("expert")
    choice, sel, send, spill = pack(
        expert_at.reshape(1).astype(jnp.int32),
        routes.reshape(1, pairs),
        tokens,
        grad_hidden.reshape(pairs, grad_hidden.shape[2]),
    )
    choice = choice.reshape(128)
    w_gate = pltpu.with_memory_space_constraint(w_gate, pltpu.HBM)
    w_up = pltpu.with_memory_space_constraint(w_up, pltpu.HBM)
    ups = [(e, (e + 2) % EXPERTS) for e in range(EXPERTS)]
    downs = [(e, (e - 2) % EXPERTS) for e in range(EXPERTS)]
    beside = [(e, e ^ 1) for e in range(EXPERTS)]
    column = [spill]
    right = left = spill
    for _ in range(3):
        right = lax.ppermute(right, "expert", ups)
        left = lax.ppermute(left, "expert", downs)
        column += [right, left]
    column.append(lax.ppermute(right, "expert", ups))
    pieces = [
        lax.ppermute(choose(choice, column[a:b]), "expert", beside) for a, b in PIECES
    ]
    send, right, left = lax.optimization_barrier((send, right, left))
    got = lax.all_to_all(send, "expert", split_axis=0, concat_axis=0, tiled=True)
    over_x, over_g, over_u, back = over(choice, column, pieces, w_gate, w_up)
    delta_g, delta_u, back = direct(got, w_gate, w_up, back)
    returned = lax.all_to_all(back, "expert", split_axis=0, concat_axis=0, tiled=True)
    rows = (got, delta_g, delta_u, over_x, over_g, over_u)

    keep_table = np.array([[partner(i, s) for s in range(steps)] for i in range(groups)], np.int32)
    me = lax.axis_index("dp")
    keep_blocks = jnp.asarray(keep_table)[me]
    other_half = weight_send(keep_blocks ^ 1, rows)
    came = lax.ppermute(other_half, "dp", [(i, i ^ 1) for i in range(groups)])
    own, *parts = weight_keep(keep_blocks, rows, came)
    total = own
    for s, part in enumerate(parts, 1):
        came = lax.ppermute(part, "dp", [(i, partner(i, s)) for i in range(groups)])
        total = total + came.astype(jnp.float32)
    grad_tokens = lax.dot_general(
        sel, returned, (((0,), (0,)), ((), ())), preferred_element_type=jnp.float32
    ).astype(jnp.bfloat16)
    return grad_tokens, total[None, :, :FF], total[None, :, FF:]


def solution(mesh):
    placed = (
        P(("dp", "expert"), None),
        P(("dp", "expert"), None),
        P(("dp", "expert"), None, None),
        P("expert", None, None),
        P("expert", None, None),
    )
    return jax.shard_map(
        per_device,
        mesh=mesh,
        in_specs=placed,
        out_specs=(P(("dp", "expert"), None), P("expert", "dp", None), P("expert", "dp", None)),
        check_vma=False,
    )
```

```python
import functools

import jax
import jax.numpy as jnp
import numpy as np
from jax import lax
from jax.experimental import pallas as pl
from jax.experimental.pallas import tpu as pltpu
from jax.sharding import PartitionSpec as P

D = 2048
FF = 768
EXPERTS = 16
COLD = 16
SPILL = 32
CAP = COLD + SPILL
ROWS = EXPERTS * CAP
DIRECT = EXPERTS * COLD
OVER = EXPERTS * SPILL
WIDTH = D + FF
OFFSETS = (0, -1, 1, -2, 2, -3, 3, 4)
PIECES = ((0, 3), (3, 5))
SLOT_ME, HOT_ME, SLOT_BESIDE, ME = range(4)
HOPS = ((0, 1, False), (1, -1, False), (0, 2, False), (0, 1, True), (1, -1, True), (1, -2, True))
SLOT_HOP = 4
BLOCK = 128
FF_BLOCK = 256
MIB = 1 << 20


def target(expert, step, crosses):
    there = (expert + 2 * step + EXPERTS) % EXPERTS
    return there + 1 - 2 * (there % 2) if crosses else there


def pack_kernel(
    me_ref, routes_ref, tokens_ref, grads_ref, choice_ref, sel_ref, out_ref, over_ref
):
    pairs = routes_ref.shape[1]
    toks = tokens_ref.shape[0]
    me = me_ref[0]
    routes = routes_ref[...]
    member = (routes == lax.broadcasted_iota(jnp.int32, (EXPERTS, pairs), 0)).astype(jnp.float32)
    member_low = member.astype(jnp.bfloat16)
    earlier = (
        lax.broadcasted_iota(jnp.int32, (pairs, pairs), 0)
        < lax.broadcasted_iota(jnp.int32, (pairs, pairs), 1)
    ).astype(jnp.bfloat16)
    before = jnp.dot(member_low, earlier, preferred_element_type=jnp.float32)
    rank = jnp.sum(member * before, axis=0, keepdims=True).astype(jnp.int32)

    count_col = jnp.sum(member, axis=1, keepdims=True)
    count_row = lax.dot_general(
        jnp.ones((8, pairs), jnp.bfloat16),
        member_low,
        (((1,), (1,)), ((), ())),
        preferred_element_type=jnp.float32,
    )[:1]
    down = lax.broadcasted_iota(jnp.int32, (EXPERTS, EXPERTS), 0)
    across = lax.broadcasted_iota(jnp.int32, (EXPERTS, EXPERTS), 1)
    above_col = jnp.sum((count_row > count_col).astype(jnp.float32), axis=1, keepdims=True)
    above_row = jnp.sum((count_col > count_row).astype(jnp.float32), axis=0, keepdims=True)
    hot_col = (above_col < 1.5).astype(jnp.float32)
    hot_row = (above_row < 1.5).astype(jnp.float32)
    which_col = jnp.sum(hot_row * (across < down).astype(jnp.float32), axis=1, keepdims=True)
    which_row = jnp.sum(hot_col * (down < across).astype(jnp.float32), axis=0, keepdims=True)
    which = jnp.sum(member * which_col, axis=0, keepdims=True).astype(jnp.int32)

    lane16 = lax.broadcasted_iota(jnp.int32, (1, EXPERTS), 1)

    def at_expert(expert, row):
        return jnp.sum(
            jnp.where(lane16 == expert, row, 0.0), axis=1, keepdims=True
        ).astype(jnp.int32)

    slots = hot_row * which_row
    values = {
        SLOT_ME: at_expert(me, slots),
        HOT_ME: at_expert(me, hot_row),
        SLOT_BESIDE: at_expert(target(me, 0, True), slots),
        ME: me,
    }
    for k, (_, step, crosses) in enumerate(HOPS):
        values[SLOT_HOP + k] = at_expert(target(me, step, crosses), slots)
    lane = lax.broadcasted_iota(jnp.int32, (1, 128), 1)
    choice = jnp.zeros((1, 128), jnp.int32)
    for at, value in values.items():
        choice = jnp.where(lane == at, value, choice)
    choice_ref[...] = choice

    to_token = (
        lax.broadcasted_iota(jnp.int32, (pairs, toks), 0) // 2
        == lax.broadcasted_iota(jnp.int32, (pairs, toks), 1)
    ).astype(jnp.bfloat16)

    def picked(slot, rows):
        pick = (slot == lax.broadcasted_iota(jnp.int32, (rows, pairs), 0)).astype(jnp.bfloat16)
        tok = jnp.dot(pick, to_token, preferred_element_type=jnp.float32).astype(jnp.bfloat16)
        return pick, tok

    def fill(ref, slot):
        pick, tok = picked(slot, ref.shape[0])
        ref[:, :D] = jnp.dot(tok, tokens_ref[...], preferred_element_type=jnp.float32).astype(
            jnp.bfloat16
        )
        ref[:, D:] = jnp.dot(pick, grads_ref[...], preferred_element_type=jnp.float32).astype(
            jnp.bfloat16
        )

    fill(over_ref, jnp.where(rank >= COLD, which * SPILL + rank - COLD, -1))
    fill(out_ref, jnp.where(rank < COLD, routes * COLD + rank, -1))
    sel_ref[...] = picked(routes * CAP + rank, ROWS)[1]


def pack(me, routes, tokens, grads):
    toks, pairs = tokens.shape[0], grads.shape[0]
    vmem = pl.BlockSpec(memory_space=pltpu.VMEM)
    return pl.pallas_call(
        pack_kernel,
        in_specs=[pl.BlockSpec(memory_space=pltpu.SMEM), vmem, vmem, vmem],
        out_specs=[vmem] * 4,
        out_shape=[
            jax.ShapeDtypeStruct((1, 128), jnp.int32),
            jax.ShapeDtypeStruct((ROWS, toks), jnp.bfloat16),
            jax.ShapeDtypeStruct((DIRECT, WIDTH), jnp.bfloat16),
            jax.ShapeDtypeStruct((2 * SPILL, WIDTH), jnp.bfloat16),
        ],
        compiler_params=pltpu.CompilerParams(vmem_limit_bytes=12 * MIB),
        cost_estimate=pl.CostEstimate(flops=10**9, bytes_accessed=4 * MIB, transcendentals=0),
        name="pack",
    )(me, routes, tokens, grads)


def choose_kernel(choice_ref, *refs):
    for k, ref in enumerate(refs[:-1]):
        refs[-1][k * SPILL : (k + 1) * SPILL, :] = ref[...]


def choose(choice, blocks):
    count = len(blocks)
    return pl.pallas_call(
        choose_kernel,
        grid_spec=pltpu.PrefetchScalarGridSpec(
            num_scalar_prefetch=1,
            grid=(1,),
            in_specs=[pl.BlockSpec((SPILL, WIDTH), lambda i, c: (c[SLOT_BESIDE], 0))] * count,
            out_specs=pl.BlockSpec((count * SPILL, WIDTH), lambda i, c: (0, 0)),
        ),
        out_shape=jax.ShapeDtypeStruct((count * SPILL, WIDTH), jnp.bfloat16),
        compiler_params=pltpu.CompilerParams(vmem_limit_bytes=4 * MIB),
        cost_estimate=pl.CostEstimate(
            flops=0, bytes_accessed=4 * count * SPILL * WIDTH, transcendentals=0
        ),
        name="choose",
    )(choice, *blocks)


def hop_kernel(choice_ref, *refs):
    for k in range(len(HOPS)):
        refs[len(HOPS) + k][...] = refs[k][...]


def hop_rows(choice, blocks):
    return pl.pallas_call(
        hop_kernel,
        grid_spec=pltpu.PrefetchScalarGridSpec(
            num_scalar_prefetch=1,
            grid=(1,),
            in_specs=[
                pl.BlockSpec((SPILL, WIDTH), lambda i, c, k=k: (c[SLOT_HOP + k], 0))
                for k in range(len(HOPS))
            ],
            out_specs=[pl.BlockSpec((SPILL, WIDTH), lambda i, c: (0, 0))] * len(HOPS),
        ),
        out_shape=[jax.ShapeDtypeStruct((SPILL, WIDTH), jnp.bfloat16)] * len(HOPS),
        compiler_params=pltpu.CompilerParams(vmem_limit_bytes=6 * MIB),
        cost_estimate=pl.CostEstimate(
            flops=0, bytes_accessed=4 * len(HOPS) * SPILL * WIDTH, transcendentals=0
        ),
        name="hop_rows",
    )(choice, *[blocks[from_above] for from_above, _, _ in HOPS])


def deltas(x, dh, wg, wu):
    gate = jnp.dot(x, wg, preferred_element_type=jnp.float32)
    up = jnp.dot(x, wu, preferred_element_type=jnp.float32)
    sig = jax.nn.sigmoid(gate)
    wide = dh.astype(jnp.float32)
    delta_g = (wide * up * sig * (1.0 + gate * (1.0 - sig))).astype(jnp.bfloat16)
    delta_u = (wide * gate * sig).astype(jnp.bfloat16)
    return delta_g, delta_u


def back_rows(delta_g, delta_u, wg, wu):
    dims = (((1,), (1,)), ((), ()))
    return lax.dot_general(
        delta_g, wg, dims, preferred_element_type=jnp.float32
    ) + lax.dot_general(delta_u, wu, dims, preferred_element_type=jnp.float32)


def over_kernel(choice_ref, *refs):
    inputs = 5 + len(PIECES) + len(HOPS)
    wg_ref, wu_ref, x_ref, delta_g_ref, delta_u_ref, back_ref, acc_ref, dh_ref = refs[inputs:]
    j = pl.program_id(0)
    last = pl.num_programs(0) - 1
    hot = choice_ref[HOT_ME] == 1

    @pl.when(j == 0)
    def _():
        back_ref[...] = jnp.zeros_like(back_ref)
        at = 0
        for ref in refs[:inputs]:
            rows = ref.shape[0]
            x_ref[at : at + rows, :] = ref[:, :D]
            for k in range(FF // FF_BLOCK):
                dh_ref[k, at : at + rows, :] = ref[
                    :, D + k * FF_BLOCK : D + (k + 1) * FF_BLOCK
                ]
            at += rows

    @pl.when(jnp.logical_not(hot))
    def _():
        delta_g_ref[...] = jnp.zeros_like(delta_g_ref)
        delta_u_ref[...] = jnp.zeros_like(delta_u_ref)

    @pl.when(hot)
    def _():
        delta_g, delta_u = deltas(x_ref[...], dh_ref[j], wg_ref[0], wu_ref[0])
        delta_g_ref[...] = delta_g
        delta_u_ref[...] = delta_u
        part = back_rows(delta_g, delta_u, wg_ref[0], wu_ref[0])

        @pl.when(j == 0)
        def _():
            acc_ref[...] = part

        @pl.when(jnp.logical_and(j > 0, j < last))
        def _():
            acc_ref[...] += part

        @pl.when(j == last)
        def _():
            acc_ref[...] += part
            me = choice_ref[ME]
            for k in range(2 * len(OFFSETS)):
                source = (me + 2 * OFFSETS[k % 8] + EXPERTS) % EXPERTS
                if k >= 8:
                    source = source + 1 - 2 * (source % 2)
                row = pl.multiple_of(source * CAP + COLD, COLD)
                back_ref[pl.ds(row, SPILL), :] = acc_ref[
                    k * SPILL : (k + 1) * SPILL, :
                ].astype(jnp.bfloat16)


def over(choice, column, rest, w_gate, w_up):
    steps = FF // FF_BLOCK

    def whole(a):
        return pl.BlockSpec(a.shape, lambda j, c: (0, 0))

    return pl.pallas_call(
        over_kernel,
        grid_spec=pltpu.PrefetchScalarGridSpec(
            num_scalar_prefetch=1,
            grid=(steps,),
            in_specs=[pl.BlockSpec((SPILL, WIDTH), lambda j, c: (c[SLOT_ME], 0))] * len(column)
            + [whole(a) for a in rest]
            + [pl.BlockSpec((1, D, FF_BLOCK), lambda j, c: (0, 0, j))] * 2,
            out_specs=[
                pl.BlockSpec((OVER, D), lambda j, c: (0, 0)),
                pl.BlockSpec((OVER, FF_BLOCK), lambda j, c: (0, j)),
                pl.BlockSpec((OVER, FF_BLOCK), lambda j, c: (0, j)),
                pl.BlockSpec((ROWS, D), lambda j, c: (0, 0)),
            ],
            scratch_shapes=[
                pltpu.VMEM((OVER, D), jnp.float32),
                pltpu.VMEM((steps, OVER, FF_BLOCK), jnp.bfloat16),
            ],
        ),
        out_shape=[
            jax.ShapeDtypeStruct((OVER, D), jnp.bfloat16),
            jax.ShapeDtypeStruct((OVER, FF), jnp.bfloat16),
            jax.ShapeDtypeStruct((OVER, FF), jnp.bfloat16),
            pltpu.HBM((ROWS, D), jnp.bfloat16),
        ],
        compiler_params=pltpu.CompilerParams(vmem_limit_bytes=34 * MIB),
        cost_estimate=pl.CostEstimate(
            flops=8 * OVER * D * FF, bytes_accessed=17 * MIB, transcendentals=OVER * FF
        ),
        name="over",
    )(choice, *column, *rest, w_gate, w_up)


def direct_kernel(
    x_ref, dh_ref, wg_ref, wu_ref, old_ref, delta_g_ref, delta_u_ref, back_ref, acc_ref, low_ref, sems
):
    j = pl.program_id(0)
    delta_g, delta_u = deltas(x_ref[...], dh_ref[...], wg_ref[0], wu_ref[0])
    part = back_rows(delta_g, delta_u, wg_ref[0], wu_ref[0])
    delta_g_ref[...] = delta_g
    delta_u_ref[...] = delta_u
    last = pl.num_programs(0) - 1

    @pl.when(j == 0)
    def _():
        acc_ref[...] = part

    @pl.when(jnp.logical_and(j > 0, j < last))
    def _():
        acc_ref[...] += part

    @pl.when(j == last)
    def _():
        low_ref[...] = (acc_ref[...] + part).astype(jnp.bfloat16)
        copies = [
            pltpu.make_async_copy(
                low_ref.at[pl.ds(e * COLD, COLD), :],
                back_ref.at[pl.ds(e * CAP, COLD), :],
                sems.at[e],
            )
            for e in range(EXPERTS)
        ]
        for copy in copies:
            copy.start()
        for copy in copies:
            copy.wait()


def direct(got, w_gate, w_up, back):
    steps = FF // FF_BLOCK
    off = D // FF_BLOCK
    return pl.pallas_call(
        direct_kernel,
        grid=(steps,),
        in_specs=[
            pl.BlockSpec((DIRECT, D), lambda j: (0, 0)),
            pl.BlockSpec((DIRECT, FF_BLOCK), lambda j: (0, off + j)),
            pl.BlockSpec((1, D, FF_BLOCK), lambda j: (0, 0, j)),
            pl.BlockSpec((1, D, FF_BLOCK), lambda j: (0, 0, j)),
            pl.BlockSpec(memory_space=pltpu.HBM),
        ],
        out_specs=[
            pl.BlockSpec((DIRECT, FF_BLOCK), lambda j: (0, j)),
            pl.BlockSpec((DIRECT, FF_BLOCK), lambda j: (0, j)),
            pl.BlockSpec(memory_space=pltpu.HBM),
        ],
        out_shape=[
            jax.ShapeDtypeStruct((DIRECT, FF), jnp.bfloat16),
            jax.ShapeDtypeStruct((DIRECT, FF), jnp.bfloat16),
            pltpu.HBM((ROWS, D), jnp.bfloat16),
        ],
        scratch_shapes=[
            pltpu.VMEM((DIRECT, D), jnp.float32),
            pltpu.VMEM((DIRECT, D), jnp.bfloat16),
            pltpu.SemaphoreType.DMA((EXPERTS,)),
        ],
        input_output_aliases={4: 2},
        compiler_params=pltpu.CompilerParams(vmem_limit_bytes=20 * MIB),
        cost_estimate=pl.CostEstimate(
            flops=8 * DIRECT * D * FF, bytes_accessed=10 * MIB, transcendentals=DIRECT * FF
        ),
        name="direct",
    )(got, got, w_gate, w_up, pltpu.with_memory_space_constraint(back, pltpu.HBM))


def weight_part(x_ref, dg_ref, du_ref, over_x_ref, over_dg_ref, over_du_ref):
    dims = (((0,), (0,)), ((), ()))
    x = x_ref[...]
    over_x = over_x_ref[...]

    def both(d_ref, over_d_ref):
        return lax.dot_general(
            x, d_ref[...], dims, preferred_element_type=jnp.float32
        ) + lax.dot_general(over_x, over_d_ref[...], dims, preferred_element_type=jnp.float32)

    return both(dg_ref, over_dg_ref), both(du_ref, over_du_ref)


def weight_send_kernel(block_ref, *refs):
    gate, up = weight_part(*refs[:6])
    out_ref = refs[6]
    out_ref[:, :FF] = gate.astype(jnp.bfloat16)
    out_ref[:, FF:] = up.astype(jnp.bfloat16)


def weight_specs():
    return [
        pl.BlockSpec((DIRECT, BLOCK), lambda i, b: (0, b[i])),
        pl.BlockSpec((DIRECT, FF), lambda i, b: (0, 0)),
        pl.BlockSpec((DIRECT, FF), lambda i, b: (0, 0)),
        pl.BlockSpec((OVER, BLOCK), lambda i, b: (0, b[i])),
        pl.BlockSpec((OVER, FF), lambda i, b: (0, 0)),
        pl.BlockSpec((OVER, FF), lambda i, b: (0, 0)),
    ]


def weight_send(blocks, rows):
    count = blocks.shape[0]
    return pl.pallas_call(
        weight_send_kernel,
        grid_spec=pltpu.PrefetchScalarGridSpec(
            num_scalar_prefetch=1,
            grid=(count,),
            in_specs=weight_specs(),
            out_specs=pl.BlockSpec((BLOCK, 2 * FF), lambda i, b: (i, 0)),
        ),
        out_shape=jax.ShapeDtypeStruct((count * BLOCK, 2 * FF), jnp.bfloat16),
        compiler_params=pltpu.CompilerParams(vmem_limit_bytes=18 * MIB),
        cost_estimate=pl.CostEstimate(
            flops=4 * ROWS * count * BLOCK * FF, bytes_accessed=8 * MIB, transcendentals=0
        ),
        name="weight_send",
    )(blocks, *rows)


def weight_keep_kernel(block_ref, *refs):
    i = pl.program_id(0)
    came_ref, own_ref, *out_refs = refs[6:]
    gate, up = weight_part(*refs[:6])
    gate = gate + came_ref[:, :FF].astype(jnp.float32)
    up = up + came_ref[:, FF:].astype(jnp.float32)

    @pl.when(i == 0)
    def _():
        own_ref[:, :FF] = gate
        own_ref[:, FF:] = up

    for k, out_ref in enumerate(out_refs):

        @pl.when(i == k + 1)
        def _(out_ref=out_ref):
            out_ref[:, :FF] = gate.astype(jnp.bfloat16)
            out_ref[:, FF:] = up.astype(jnp.bfloat16)


def weight_keep(blocks, rows, came):
    count = blocks.shape[0]
    whole = pl.BlockSpec((BLOCK, 2 * FF), lambda i, b: (0, 0))
    return pl.pallas_call(
        weight_keep_kernel,
        grid_spec=pltpu.PrefetchScalarGridSpec(
            num_scalar_prefetch=1,
            grid=(count,),
            in_specs=weight_specs() + [pl.BlockSpec((BLOCK, 2 * FF), lambda i, b: (i, 0))],
            out_specs=[whole] * count,
        ),
        out_shape=[jax.ShapeDtypeStruct((BLOCK, 2 * FF), jnp.float32)]
        + [jax.ShapeDtypeStruct((BLOCK, 2 * FF), jnp.bfloat16)] * (count - 1),
        compiler_params=pltpu.CompilerParams(vmem_limit_bytes=24 * MIB),
        cost_estimate=pl.CostEstimate(
            flops=4 * ROWS * count * BLOCK * FF, bytes_accessed=11 * MIB, transcendentals=0
        ),
        name="weight_keep",
    )(blocks, *rows, came)


def place(index):
    return index // 4, index // 2 % 2, index % 2


def partner(index, step):
    y, x, core = place(index)
    return (y + step // 2) % 4 * 4 + (x + step % 2) % 2 * 2 + core


def per_device(tokens, routes, grad_hidden, w_gate, w_up):
    toks, per_token = routes.shape
    pairs = toks * per_token
    groups = lax.axis_size("dp")
    steps = groups // 2
    expert_at = lax.axis_index("expert")
    choice, sel, send, spill = pack(
        expert_at.reshape(1).astype(jnp.int32),
        routes.reshape(1, pairs),
        tokens,
        grad_hidden.reshape(pairs, grad_hidden.shape[2]),
    )
    choice = choice.reshape(128)
    w_gate = pltpu.with_memory_space_constraint(w_gate, pltpu.HBM)
    w_up = pltpu.with_memory_space_constraint(w_up, pltpu.HBM)
    ups = [(e, (e + 2) % EXPERTS) for e in range(EXPERTS)]
    downs = [(e, (e - 2) % EXPERTS) for e in range(EXPERTS)]
    beside = [(e, e ^ 1) for e in range(EXPERTS)]

    column = [spill]
    right = left = spill
    for _ in range(2):
        right = lax.ppermute(right, "expert", ups)
        left = lax.ppermute(left, "expert", downs)
        column += [right, left]
    hops = [
        lax.ppermute(
            block, "expert", [(e, target(e, step, crosses)) for e in range(EXPERTS)]
        )
        for block, (_, step, crosses) in zip(hop_rows(choice, (right, left)), HOPS)
    ]
    pieces = [lax.ppermute(choose(choice, column[a:b]), "expert", beside) for a, b in PIECES]
    rest = [*hops[:3], *pieces, *hops[3:]]
    send, *rest = lax.optimization_barrier((send, *rest))
    got = lax.all_to_all(send, "expert", split_axis=0, concat_axis=0, tiled=True)
    over_x, over_g, over_u, back = over(choice, column, rest, w_gate, w_up)
    delta_g, delta_u, back = direct(got, w_gate, w_up, back)
    returned = lax.all_to_all(back, "expert", split_axis=0, concat_axis=0, tiled=True)
    rows = (got, delta_g, delta_u, over_x, over_g, over_u)

    keep_table = np.array([[partner(i, s) for s in range(steps)] for i in range(groups)], np.int32)
    me = lax.axis_index("dp")
    keep_blocks = jnp.asarray(keep_table)[me]
    other_half = weight_send(keep_blocks ^ 1, rows)
    came = lax.ppermute(other_half, "dp", [(i, i ^ 1) for i in range(groups)])
    own, *parts = weight_keep(keep_blocks, rows, came)
    total = own
    for s, part in enumerate(parts, 1):
        came = lax.ppermute(part, "dp", [(i, partner(i, s)) for i in range(groups)])
        total = total + came.astype(jnp.float32)
    grad_tokens = lax.dot_general(
        sel, returned, (((0,), (0,)), ((), ())), preferred_element_type=jnp.float32
    ).astype(jnp.bfloat16)
    return grad_tokens, total[None, :, :FF], total[None, :, FF:]


def solution(mesh):
    placed = (
        P(("dp", "expert"), None),
        P(("dp", "expert"), None),
        P(("dp", "expert"), None, None),
        P("expert", None, None),
        P("expert", None, None),
    )
    return jax.shard_map(
        per_device,
        mesh=mesh,
        in_specs=placed,
        out_specs=(P(("dp", "expert"), None), P("expert", "dp", None), P("expert", "dp", None)),
        check_vma=False,
    )
```

```python
import functools

import jax
import jax.numpy as jnp
import numpy as np
from jax import lax
from jax.experimental import pallas as pl
from jax.experimental.pallas import tpu as pltpu
from jax.sharding import PartitionSpec as P

D = 2048
FF = 768
EXPERTS = 16
COLD = 16
SPILL = 32
CAP = COLD + SPILL
ROWS = EXPERTS * CAP
DIRECT = EXPERTS * COLD
OVER = EXPERTS * SPILL
WIDTH = D + FF
OFFSETS = (0, -1, 1, -2, 2, -3, 3, 4)
PIECES = ((0, 3), (3, 5))
SLOT_ME, HOT_ME, SLOT_BESIDE, ME = range(4)
HOPS = ((0, 1, False), (1, -1, False), (0, 2, False), (0, 1, True), (1, -1, True), (1, -2, True))
SLOT_HOP = 4
BLOCK = 128
FF_BLOCK = 256
MIB = 1 << 20


def target(expert, step, crosses):
    there = (expert + 2 * step + EXPERTS) % EXPERTS
    return there + 1 - 2 * (there % 2) if crosses else there


def in_hbm(a):
    return pltpu.with_memory_space_constraint(a, pltpu.HBM)


def pack_kernel(
    me_ref, routes_ref, tokens_ref, grads_ref, choice_ref, sel_ref, out_ref, over_ref
):
    pairs = routes_ref.shape[1]
    toks = tokens_ref.shape[0]
    me = me_ref[0]
    routes = routes_ref[...]
    member = (routes == lax.broadcasted_iota(jnp.int32, (EXPERTS, pairs), 0)).astype(jnp.float32)
    member_low = member.astype(jnp.bfloat16)
    earlier = (
        lax.broadcasted_iota(jnp.int32, (pairs, pairs), 0)
        < lax.broadcasted_iota(jnp.int32, (pairs, pairs), 1)
    ).astype(jnp.bfloat16)
    before = jnp.dot(member_low, earlier, preferred_element_type=jnp.float32)
    rank = jnp.sum(member * before, axis=0, keepdims=True).astype(jnp.int32)

    count_col = jnp.sum(member, axis=1, keepdims=True)
    count_row = lax.dot_general(
        jnp.ones((8, pairs), jnp.bfloat16),
        member_low,
        (((1,), (1,)), ((), ())),
        preferred_element_type=jnp.float32,
    )[:1]
    down = lax.broadcasted_iota(jnp.int32, (EXPERTS, EXPERTS), 0)
    across = lax.broadcasted_iota(jnp.int32, (EXPERTS, EXPERTS), 1)
    above_col = jnp.sum((count_row > count_col).astype(jnp.float32), axis=1, keepdims=True)
    above_row = jnp.sum((count_col > count_row).astype(jnp.float32), axis=0, keepdims=True)
    hot_col = (above_col < 1.5).astype(jnp.float32)
    hot_row = (above_row < 1.5).astype(jnp.float32)
    which_col = jnp.sum(hot_row * (across < down).astype(jnp.float32), axis=1, keepdims=True)
    which_row = jnp.sum(hot_col * (down < across).astype(jnp.float32), axis=0, keepdims=True)
    which = jnp.sum(member * which_col, axis=0, keepdims=True).astype(jnp.int32)

    lane16 = lax.broadcasted_iota(jnp.int32, (1, EXPERTS), 1)

    def at_expert(expert, row):
        return jnp.sum(
            jnp.where(lane16 == expert, row, 0.0), axis=1, keepdims=True
        ).astype(jnp.int32)

    slots = hot_row * which_row
    values = {
        SLOT_ME: at_expert(me, slots),
        HOT_ME: at_expert(me, hot_row),
        SLOT_BESIDE: at_expert(target(me, 0, True), slots),
        ME: me,
    }
    for k, (_, step, crosses) in enumerate(HOPS):
        values[SLOT_HOP + k] = at_expert(target(me, step, crosses), slots)
    lane = lax.broadcasted_iota(jnp.int32, (1, 128), 1)
    choice = jnp.zeros((1, 128), jnp.int32)
    for at, value in values.items():
        choice = jnp.where(lane == at, value, choice)
    choice_ref[...] = choice

    to_token = (
        lax.broadcasted_iota(jnp.int32, (pairs, toks), 0) // 2
        == lax.broadcasted_iota(jnp.int32, (pairs, toks), 1)
    ).astype(jnp.bfloat16)

    def picked(slot, rows):
        pick = (slot == lax.broadcasted_iota(jnp.int32, (rows, pairs), 0)).astype(jnp.bfloat16)
        tok = jnp.dot(pick, to_token, preferred_element_type=jnp.float32).astype(jnp.bfloat16)
        return pick, tok

    def fill(ref, slot):
        pick, tok = picked(slot, ref.shape[0])
        ref[:, :D] = jnp.dot(tok, tokens_ref[...], preferred_element_type=jnp.float32).astype(
            jnp.bfloat16
        )
        ref[:, D:] = jnp.dot(pick, grads_ref[...], preferred_element_type=jnp.float32).astype(
            jnp.bfloat16
        )

    fill(over_ref, jnp.where(rank >= COLD, which * SPILL + rank - COLD, -1))
    fill(out_ref, jnp.where(rank < COLD, routes * COLD + rank, -1))
    back = routes * CAP + rank == lax.broadcasted_iota(jnp.int32, (ROWS, pairs), 0)
    of_token = (
        lax.broadcasted_iota(jnp.int32, (toks, pairs), 1) // 2
        == lax.broadcasted_iota(jnp.int32, (toks, pairs), 0)
    ).astype(jnp.bfloat16)
    sel_ref[...] = lax.dot_general(
        of_token,
        back.astype(jnp.bfloat16),
        (((1,), (1,)), ((), ())),
        preferred_element_type=jnp.float32,
    ).astype(jnp.bfloat16)


def pack(me, routes, tokens, grads):
    toks, pairs = tokens.shape[0], grads.shape[0]
    vmem = pl.BlockSpec(memory_space=pltpu.VMEM)
    return pl.pallas_call(
        pack_kernel,
        in_specs=[pl.BlockSpec(memory_space=pltpu.SMEM), vmem, vmem, vmem],
        out_specs=[vmem] * 4,
        out_shape=[
            jax.ShapeDtypeStruct((1, 128), jnp.int32),
            pltpu.HBM((toks, ROWS), jnp.bfloat16),
            jax.ShapeDtypeStruct((DIRECT, WIDTH), jnp.bfloat16),
            jax.ShapeDtypeStruct((2 * SPILL, WIDTH), jnp.bfloat16),
        ],
        compiler_params=pltpu.CompilerParams(vmem_limit_bytes=12 * MIB),
        cost_estimate=pl.CostEstimate(flops=10**9, bytes_accessed=4 * MIB, transcendentals=0),
        name="pack",
    )(me, routes, tokens, grads)


def choose_kernel(choice_ref, *refs):
    for k, ref in enumerate(refs[:-1]):
        refs[-1][k * SPILL : (k + 1) * SPILL, :] = ref[...]


def choose(choice, blocks):
    count = len(blocks)
    return pl.pallas_call(
        choose_kernel,
        grid_spec=pltpu.PrefetchScalarGridSpec(
            num_scalar_prefetch=1,
            grid=(1,),
            in_specs=[pl.BlockSpec((SPILL, WIDTH), lambda i, c: (c[SLOT_BESIDE], 0))] * count,
            out_specs=pl.BlockSpec((count * SPILL, WIDTH), lambda i, c: (0, 0)),
        ),
        out_shape=jax.ShapeDtypeStruct((count * SPILL, WIDTH), jnp.bfloat16),
        compiler_params=pltpu.CompilerParams(vmem_limit_bytes=4 * MIB),
        cost_estimate=pl.CostEstimate(
            flops=0, bytes_accessed=4 * count * SPILL * WIDTH, transcendentals=0
        ),
        name="choose",
    )(choice, *blocks)


def hop_kernel(choice_ref, *refs):
    for k in range(len(HOPS)):
        refs[len(HOPS) + k][...] = refs[k][...]


def hop_rows(choice, blocks):
    return pl.pallas_call(
        hop_kernel,
        grid_spec=pltpu.PrefetchScalarGridSpec(
            num_scalar_prefetch=1,
            grid=(1,),
            in_specs=[
                pl.BlockSpec((SPILL, WIDTH), lambda i, c, k=k: (c[SLOT_HOP + k], 0))
                for k in range(len(HOPS))
            ],
            out_specs=[pl.BlockSpec((SPILL, WIDTH), lambda i, c: (0, 0))] * len(HOPS),
        ),
        out_shape=[jax.ShapeDtypeStruct((SPILL, WIDTH), jnp.bfloat16)] * len(HOPS),
        compiler_params=pltpu.CompilerParams(vmem_limit_bytes=6 * MIB),
        cost_estimate=pl.CostEstimate(
            flops=0, bytes_accessed=4 * len(HOPS) * SPILL * WIDTH, transcendentals=0
        ),
        name="hop_rows",
    )(choice, *[blocks[from_above] for from_above, _, _ in HOPS])


def deltas(x, dh, wg, wu):
    gate = jnp.dot(x, wg, preferred_element_type=jnp.float32)
    up = jnp.dot(x, wu, preferred_element_type=jnp.float32)
    sig = jax.nn.sigmoid(gate)
    wide = dh.astype(jnp.float32)
    delta_g = (wide * up * sig * (1.0 + gate * (1.0 - sig))).astype(jnp.bfloat16)
    delta_u = (wide * gate * sig).astype(jnp.bfloat16)
    return delta_g, delta_u


def put_deltas(ref, j, delta_g, delta_u):
    for first, delta in ((0, delta_g), (FF, delta_u)):
        ref[:, pl.ds(pl.multiple_of(first + j * FF_BLOCK, FF_BLOCK), FF_BLOCK)] = delta


def back_rows(delta_g, delta_u, wg, wu):
    dims = (((1,), (1,)), ((), ()))
    return lax.dot_general(
        delta_g, wg, dims, preferred_element_type=jnp.float32
    ) + lax.dot_general(delta_u, wu, dims, preferred_element_type=jnp.float32)


def over_kernel(choice_ref, *refs):
    inputs = 5 + len(PIECES) + len(HOPS)
    wg_ref, wu_ref, x_ref, delta_ref, back_ref, acc_ref, dh_ref = refs[inputs:]
    j = pl.program_id(0)
    last = pl.num_programs(0) - 1
    hot = choice_ref[HOT_ME] == 1

    @pl.when(j == 0)
    def _():
        back_ref[...] = jnp.zeros_like(back_ref)
        at = 0
        for ref in refs[:inputs]:
            rows = ref.shape[0]
            x_ref[at : at + rows, :] = ref[:, :D]
            for k in range(FF // FF_BLOCK):
                dh_ref[k, at : at + rows, :] = ref[
                    :, D + k * FF_BLOCK : D + (k + 1) * FF_BLOCK
                ]
            at += rows

    @pl.when(jnp.logical_not(hot))
    def _():
        delta_ref[...] = jnp.zeros_like(delta_ref)

    @pl.when(hot)
    def _():
        delta_g, delta_u = deltas(x_ref[...], dh_ref[j], wg_ref[0], wu_ref[0])
        put_deltas(delta_ref, j, delta_g, delta_u)
        part = back_rows(delta_g, delta_u, wg_ref[0], wu_ref[0])

        @pl.when(j == 0)
        def _():
            acc_ref[...] = part

        @pl.when(jnp.logical_and(j > 0, j < last))
        def _():
            acc_ref[...] += part

        @pl.when(j == last)
        def _():
            acc_ref[...] += part
            me = choice_ref[ME]
            for k in range(2 * len(OFFSETS)):
                source = (me + 2 * OFFSETS[k % 8] + EXPERTS) % EXPERTS
                if k >= 8:
                    source = source + 1 - 2 * (source % 2)
                row = pl.multiple_of(source * CAP + COLD, COLD)
                back_ref[pl.ds(row, SPILL), :] = acc_ref[
                    k * SPILL : (k + 1) * SPILL, :
                ].astype(jnp.bfloat16)


def over(choice, column, rest, w_gate, w_up):
    steps = FF // FF_BLOCK

    def whole(a):
        return pl.BlockSpec(a.shape, lambda j, c: (0, 0))

    return pl.pallas_call(
        over_kernel,
        grid_spec=pltpu.PrefetchScalarGridSpec(
            num_scalar_prefetch=1,
            grid=(steps,),
            in_specs=[pl.BlockSpec((SPILL, WIDTH), lambda j, c: (c[SLOT_ME], 0))] * len(column)
            + [whole(a) for a in rest]
            + [pl.BlockSpec((1, D, FF_BLOCK), lambda j, c: (0, 0, j))] * 2,
            out_specs=[
                pl.BlockSpec((OVER, D), lambda j, c: (0, 0)),
                pl.BlockSpec((OVER, 2 * FF), lambda j, c: (0, 0)),
                pl.BlockSpec((ROWS, D), lambda j, c: (0, 0)),
            ],
            scratch_shapes=[
                pltpu.VMEM((OVER, D), jnp.float32),
                pltpu.VMEM((steps, OVER, FF_BLOCK), jnp.bfloat16),
            ],
        ),
        out_shape=[
            pltpu.HBM((OVER, D), jnp.bfloat16),
            pltpu.HBM((OVER, 2 * FF), jnp.bfloat16),
            pltpu.HBM((ROWS, D), jnp.bfloat16),
        ],
        compiler_params=pltpu.CompilerParams(vmem_limit_bytes=34 * MIB),
        cost_estimate=pl.CostEstimate(
            flops=8 * OVER * D * FF, bytes_accessed=17 * MIB, transcendentals=OVER * FF
        ),
        name="over",
    )(choice, *column, *rest, w_gate, w_up)


def direct_kernel(
    x_ref, dh_ref, wg_ref, wu_ref, old_ref, delta_ref, back_ref, acc_ref, low_ref, sems
):
    j = pl.program_id(0)
    delta_g, delta_u = deltas(x_ref[...], dh_ref[...], wg_ref[0], wu_ref[0])
    part = back_rows(delta_g, delta_u, wg_ref[0], wu_ref[0])
    put_deltas(delta_ref, j, delta_g, delta_u)
    last = pl.num_programs(0) - 1

    @pl.when(j == 0)
    def _():
        acc_ref[...] = part

    @pl.when(jnp.logical_and(j > 0, j < last))
    def _():
        acc_ref[...] += part

    @pl.when(j == last)
    def _():
        low_ref[...] = (acc_ref[...] + part).astype(jnp.bfloat16)
        copies = [
            pltpu.make_async_copy(
                low_ref.at[pl.ds(e * COLD, COLD), :],
                back_ref.at[pl.ds(e * CAP, COLD), :],
                sems.at[e],
            )
            for e in range(EXPERTS)
        ]
        for copy in copies:
            copy.start()
        for copy in copies:
            copy.wait()


def direct(got, w_gate, w_up, back):
    steps = FF // FF_BLOCK
    off = D // FF_BLOCK
    return pl.pallas_call(
        direct_kernel,
        grid=(steps,),
        in_specs=[
            pl.BlockSpec((DIRECT, D), lambda j: (0, 0)),
            pl.BlockSpec((DIRECT, FF_BLOCK), lambda j: (0, off + j)),
            pl.BlockSpec((1, D, FF_BLOCK), lambda j: (0, 0, j)),
            pl.BlockSpec((1, D, FF_BLOCK), lambda j: (0, 0, j)),
            pl.BlockSpec(memory_space=pltpu.HBM),
        ],
        out_specs=[
            pl.BlockSpec((DIRECT, 2 * FF), lambda j: (0, 0)),
            pl.BlockSpec(memory_space=pltpu.HBM),
        ],
        out_shape=[
            pltpu.HBM((DIRECT, 2 * FF), jnp.bfloat16),
            pltpu.HBM((ROWS, D), jnp.bfloat16),
        ],
        scratch_shapes=[
            pltpu.VMEM((DIRECT, D), jnp.float32),
            pltpu.VMEM((DIRECT, D), jnp.bfloat16),
            pltpu.SemaphoreType.DMA((EXPERTS,)),
        ],
        input_output_aliases={4: 1},
        compiler_params=pltpu.CompilerParams(vmem_limit_bytes=20 * MIB),
        cost_estimate=pl.CostEstimate(
            flops=8 * DIRECT * D * FF, bytes_accessed=10 * MIB, transcendentals=DIRECT * FF
        ),
        name="direct",
    )(got, got, w_gate, w_up, pltpu.with_memory_space_constraint(back, pltpu.HBM))


def turned(x_ref, turned_ref, block_ref, first):
    for q in range(turned_ref.shape[0] // BLOCK):
        column = pl.multiple_of(block_ref[first + q] * BLOCK, BLOCK)
        turned_ref[q * BLOCK : (q + 1) * BLOCK, :] = x_ref[:, pl.ds(column, BLOCK)].T


def weight_over_kernel(block_ref, choice_ref, x_ref, delta_ref, out_ref, turned_ref):
    hot = choice_ref[HOT_ME] == 1

    @pl.when(hot)
    def _():
        @pl.when(pl.program_id(0) == 0)
        def _():
            turned(x_ref, turned_ref, block_ref, 0)

        out_ref[...] = jnp.dot(
            turned_ref[...], delta_ref[...], preferred_element_type=jnp.float32
        )

    @pl.when(jnp.logical_not(hot))
    def _():
        out_ref[...] = jnp.zeros_like(out_ref)


def weight_over(blocks, choice, x, delta):
    rows = blocks.shape[0] * BLOCK
    return pl.pallas_call(
        weight_over_kernel,
        grid_spec=pltpu.PrefetchScalarGridSpec(
            num_scalar_prefetch=2,
            grid=(2 * FF // FF_BLOCK,),
            in_specs=[
                pl.BlockSpec((OVER, D), lambda j, b, c: (0, 0)),
                pl.BlockSpec((OVER, FF_BLOCK), lambda j, b, c: (0, j)),
            ],
            out_specs=pl.BlockSpec((rows, FF_BLOCK), lambda j, b, c: (0, j)),
            scratch_shapes=[pltpu.VMEM((rows, OVER), jnp.bfloat16)],
        ),
        out_shape=pltpu.HBM((rows, 2 * FF), jnp.float32),
        compiler_params=pltpu.CompilerParams(vmem_limit_bytes=20 * MIB),
        cost_estimate=pl.CostEstimate(
            flops=4 * OVER * rows * FF, bytes_accessed=17 * MIB, transcendentals=0
        ),
        name="weight_over",
    )(blocks, choice, x, delta)


def weight_send_kernel(block_ref, x_ref, delta_ref, part_ref, out_ref, turned_ref):
    @pl.when(pl.program_id(0) == 0)
    def _():
        turned(x_ref, turned_ref, block_ref, 0)

    total = part_ref[...] + jnp.dot(
        turned_ref[...], delta_ref[...], preferred_element_type=jnp.float32
    )
    out_ref[...] = total.astype(jnp.bfloat16)


def weight_specs(rows, half):
    return [
        pl.BlockSpec((DIRECT, D), lambda j, b: (0, 0)),
        pl.BlockSpec((DIRECT, FF_BLOCK), lambda j, b: (0, j)),
        pl.BlockSpec((rows, FF_BLOCK), lambda j, b: (half, j)),
    ]


def weight_send(blocks, arrays):
    rows = blocks.shape[0] // 2 * BLOCK
    return pl.pallas_call(
        weight_send_kernel,
        grid_spec=pltpu.PrefetchScalarGridSpec(
            num_scalar_prefetch=1,
            grid=(2 * FF // FF_BLOCK,),
            in_specs=weight_specs(rows, 0),
            out_specs=pl.BlockSpec((rows, FF_BLOCK), lambda j, b: (0, j)),
            scratch_shapes=[pltpu.VMEM((rows, DIRECT), jnp.bfloat16)],
        ),
        out_shape=jax.ShapeDtypeStruct((rows, 2 * FF), jnp.bfloat16),
        compiler_params=pltpu.CompilerParams(vmem_limit_bytes=14 * MIB),
        cost_estimate=pl.CostEstimate(
            flops=4 * DIRECT * rows * FF, bytes_accessed=11 * MIB, transcendentals=0
        ),
        name="weight_send",
    )(blocks, *arrays)


def weight_keep_kernel(block_ref, x_ref, delta_ref, part_ref, came_ref, *refs):
    *out_refs, turned_ref = refs

    @pl.when(pl.program_id(0) == 0)
    def _():
        turned(x_ref, turned_ref, block_ref, block_ref.shape[0] // 2)

    total = jnp.dot(turned_ref[...], delta_ref[...], preferred_element_type=jnp.float32)
    total = total + part_ref[...] + came_ref[...].astype(jnp.float32)
    for k, out_ref in enumerate(out_refs):
        rows = out_ref.shape[0]
        out_ref[...] = total[k * rows : (k + 1) * rows, :].astype(out_ref.dtype)


def weight_keep(blocks, arrays, came):
    rows = blocks.shape[0] // 2 * BLOCK
    count = rows // BLOCK
    return pl.pallas_call(
        weight_keep_kernel,
        grid_spec=pltpu.PrefetchScalarGridSpec(
            num_scalar_prefetch=1,
            grid=(2 * FF // FF_BLOCK,),
            in_specs=weight_specs(rows, 1) + [pl.BlockSpec((rows, FF_BLOCK), lambda j, b: (0, j))],
            out_specs=[pl.BlockSpec((BLOCK, FF_BLOCK), lambda j, b: (0, j))] * count,
            scratch_shapes=[pltpu.VMEM((rows, DIRECT), jnp.bfloat16)],
        ),
        out_shape=[jax.ShapeDtypeStruct((BLOCK, 2 * FF), jnp.float32)] * 2
        + [jax.ShapeDtypeStruct((BLOCK, 2 * FF), jnp.bfloat16)] * (count - 2),
        compiler_params=pltpu.CompilerParams(vmem_limit_bytes=16 * MIB),
        cost_estimate=pl.CostEstimate(
            flops=4 * DIRECT * rows * FF, bytes_accessed=14 * MIB, transcendentals=0
        ),
        name="weight_keep",
    )(blocks, *arrays, came)


def place(index):
    return index // 4, index // 2 % 2, index % 2


def partner(index, step):
    y, x, core = place(index)
    return (y + step // 2) % 4 * 4 + (x + step % 2) % 2 * 2 + core


def per_device(tokens, routes, grad_hidden, w_gate, w_up):
    toks, per_token = routes.shape
    pairs = toks * per_token
    groups = lax.axis_size("dp")
    steps = groups // 2
    expert_at = lax.axis_index("expert")
    choice, sel, send, spill = pack(
        expert_at.reshape(1).astype(jnp.int32),
        routes.reshape(1, pairs),
        tokens,
        grad_hidden.reshape(pairs, grad_hidden.shape[2]),
    )
    choice = choice.reshape(128)
    w_gate, w_up = in_hbm(w_gate), in_hbm(w_up)
    ups = [(e, (e + 2) % EXPERTS) for e in range(EXPERTS)]
    downs = [(e, (e - 2) % EXPERTS) for e in range(EXPERTS)]
    beside = [(e, e ^ 1) for e in range(EXPERTS)]

    column = [spill]
    right = left = spill
    for _ in range(2):
        right = lax.ppermute(right, "expert", ups)
        left = lax.ppermute(left, "expert", downs)
        column += [right, left]
    hops = [
        lax.ppermute(
            block, "expert", [(e, target(e, step, crosses)) for e in range(EXPERTS)]
        )
        for block, (_, step, crosses) in zip(hop_rows(choice, (right, left)), HOPS)
    ]
    pieces = [lax.ppermute(choose(choice, column[a:b]), "expert", beside) for a, b in PIECES]
    rest = [*hops[:3], *pieces, *hops[3:]]
    send, *rest = lax.optimization_barrier((send, *rest))
    got = lax.all_to_all(send, "expert", split_axis=0, concat_axis=0, tiled=True)
    rest = [in_hbm(a) for a in rest]
    over_x, over_delta, back = over(choice, column, rest, w_gate, w_up)
    keep = [[partner(i, s) for s in range(steps)] for i in range(groups)]
    table = np.array([[b ^ 1 for b in row] + row for row in keep], np.int32)
    blocks = jnp.asarray(table)[lax.axis_index("dp")]
    part = weight_over(blocks, choice, in_hbm(over_x), in_hbm(over_delta))
    got, part = lax.optimization_barrier((got, part))
    delta, back = direct(got, w_gate, w_up, back)
    returned = lax.all_to_all(back, "expert", split_axis=0, concat_axis=0, tiled=True)
    rows = (got, in_hbm(delta), in_hbm(part))
    other_half = weight_send(blocks, rows)
    came = lax.ppermute(other_half, "dp", [(i, i ^ 1) for i in range(groups)])
    halves = weight_keep(blocks, rows, came)
    sums = list(halves[:2])
    for half in (1, 0):
        for s in (4, 2, 6):
            came = lax.ppermute(
                halves[s + half], "dp", [(i, partner(i, s)) for i in range(groups)]
            )
            sums[half] = sums[half] + came.astype(jnp.float32)
        if half == 1:
            across = lax.ppermute(
                sums[1].astype(jnp.bfloat16), "dp", [(i, partner(i, 1)) for i in range(groups)]
            )
    grad_tokens = jnp.dot(sel, returned, preferred_element_type=jnp.float32).astype(jnp.bfloat16)
    across, grad_tokens = lax.optimization_barrier((across, grad_tokens))
    total = sums[0] + across.astype(jnp.float32)
    return grad_tokens, total[None, :, :FF], total[None, :, FF:]


def solution(mesh):
    placed = (
        P(("dp", "expert"), None),
        P(("dp", "expert"), None),
        P(("dp", "expert"), None, None),
        P("expert", None, None),
        P("expert", None, None),
    )
    return jax.shard_map(
        per_device,
        mesh=mesh,
        in_specs=placed,
        out_specs=(P(("dp", "expert"), None), P("expert", "dp", None), P("expert", "dp", None)),
        check_vma=False,
    )
```

```python
import functools

import jax
import jax.numpy as jnp
import numpy as np
from jax import lax
from jax.experimental import pallas as pl
from jax.experimental.pallas import tpu as pltpu
from jax.sharding import PartitionSpec as P

D = 2048
FF = 768
EXPERTS = 16
COLD = 16
SPILL = 32
CAP = COLD + SPILL
ROWS = EXPERTS * CAP
DIRECT = EXPERTS * COLD
OVER = EXPERTS * SPILL
WIDTH = D + FF
OFFSETS = (0, -1, 1, -2, 2, 4, -3, 3)
PIECES = ((0, 3), (3, 5))
SLOT_ME, HOT_ME, SLOT_BESIDE, ME = range(4)
HOPS = ((0, 2, False), (1, -2, True), (0, 1, False), (1, -1, False), (0, 1, True), (1, -1, True))
SLOT_HOP = 4
BLOCK = 128
FF_BLOCK = 256
MIB = 1 << 20


def target(expert, step, crosses):
    there = (expert + 2 * step + EXPERTS) % EXPERTS
    return there + 1 - 2 * (there % 2) if crosses else there


def in_hbm(a):
    return pltpu.with_memory_space_constraint(a, pltpu.HBM)


def pack_kernel(
    me_ref,
    routes_ref,
    all_tokens_ref,
    all_grads_ref,
    choice_ref,
    sel_ref,
    out_ref,
    over_ref,
    tokens_ref,
    grads_ref,
    sems,
):
    copies = [
        pltpu.make_async_copy(all_tokens_ref, tokens_ref, sems.at[0]),
        pltpu.make_async_copy(all_grads_ref, grads_ref, sems.at[1]),
    ]
    for copy in copies:
        copy.start()
    toks = routes_ref.shape[1]
    me = me_ref[0]
    routes = [routes_ref[k : k + 1, :] for k in range(2)]
    expert_ids = lax.broadcasted_iota(jnp.int32, (EXPERTS, toks), 0)
    members = [(r == expert_ids).astype(jnp.float32) for r in routes]
    member = members[0] + members[1]
    member_low = member.astype(jnp.bfloat16)
    token_down = lax.broadcasted_iota(jnp.int32, (toks, toks), 0)
    token_across = lax.broadcasted_iota(jnp.int32, (toks, toks), 1)
    before = jnp.dot(
        member_low,
        (token_down < token_across).astype(jnp.bfloat16),
        preferred_element_type=jnp.float32,
    )

    def of_pair(table):
        return [jnp.sum(m * table, axis=0, keepdims=True).astype(jnp.int32) for m in members]

    ranks = of_pair(before)

    count_col = jnp.sum(member, axis=1, keepdims=True)
    count_row = lax.dot_general(
        jnp.ones((8, toks), jnp.bfloat16),
        member_low,
        (((1,), (1,)), ((), ())),
        preferred_element_type=jnp.float32,
    )[:1]
    down = lax.broadcasted_iota(jnp.int32, (EXPERTS, EXPERTS), 0)
    across = lax.broadcasted_iota(jnp.int32, (EXPERTS, EXPERTS), 1)
    above_col = jnp.sum((count_row > count_col).astype(jnp.float32), axis=1, keepdims=True)
    above_row = jnp.sum((count_col > count_row).astype(jnp.float32), axis=0, keepdims=True)
    hot_col = (above_col < 1.5).astype(jnp.float32)
    hot_row = (above_row < 1.5).astype(jnp.float32)
    which_col = jnp.sum(hot_row * (across < down).astype(jnp.float32), axis=1, keepdims=True)
    which_row = jnp.sum(hot_col * (down < across).astype(jnp.float32), axis=0, keepdims=True)
    whiches = of_pair(which_col)

    lane16 = lax.broadcasted_iota(jnp.int32, (1, EXPERTS), 1)

    def at_expert(expert, row):
        return jnp.sum(
            jnp.where(lane16 == expert, row, 0.0), axis=1, keepdims=True
        ).astype(jnp.int32)

    slots = hot_row * which_row
    values = {
        SLOT_ME: at_expert(me, slots),
        HOT_ME: at_expert(me, hot_row),
        SLOT_BESIDE: at_expert(target(me, 0, True), slots),
        ME: me,
    }
    for k, (_, step, crosses) in enumerate(HOPS):
        values[SLOT_HOP + k] = at_expert(target(me, step, crosses), slots)
    lane = lax.broadcasted_iota(jnp.int32, (1, 128), 1)
    choice = jnp.zeros((1, 128), jnp.int32)
    for at, value in values.items():
        choice = jnp.where(lane == at, value, choice)
    choice_ref[...] = choice

    def picked(slots, rows):
        at = lax.broadcasted_iota(jnp.int32, (rows, toks), 0)
        return [(slot == at).astype(jnp.bfloat16) for slot in slots]

    def fill(ref, slots):
        first, second = picked(slots, ref.shape[0])
        ref[:, :D] = jnp.dot(
            first + second, tokens_ref[...], preferred_element_type=jnp.float32
        ).astype(jnp.bfloat16)
        ref[:, D:] = (
            jnp.dot(first, grads_ref[0], preferred_element_type=jnp.float32)
            + jnp.dot(second, grads_ref[1], preferred_element_type=jnp.float32)
        ).astype(jnp.bfloat16)

    first, second = picked([r * CAP + rank for r, rank in zip(routes, ranks)], ROWS)
    sel_ref[...] = lax.dot_general(
        (token_down == token_across).astype(jnp.bfloat16),
        first + second,
        (((1,), (1,)), ((), ())),
        preferred_element_type=jnp.float32,
    ).astype(jnp.bfloat16)
    for copy in copies:
        copy.wait()
    fill(
        over_ref,
        [
            jnp.where(rank >= COLD, which * SPILL + rank - COLD, -1)
            for which, rank in zip(whiches, ranks)
        ],
    )
    fill(
        out_ref,
        [jnp.where(rank < COLD, r * COLD + rank, -1) for r, rank in zip(routes, ranks)],
    )


def pack(me, routes, tokens, grads):
    toks = tokens.shape[0]
    vmem = pl.BlockSpec(memory_space=pltpu.VMEM)
    hbm = pl.BlockSpec(memory_space=pltpu.HBM)
    return pl.pallas_call(
        pack_kernel,
        in_specs=[pl.BlockSpec(memory_space=pltpu.SMEM), vmem, hbm, hbm],
        out_specs=[vmem] * 4,
        out_shape=[
            jax.ShapeDtypeStruct((1, 128), jnp.int32),
            pltpu.HBM((toks, ROWS), jnp.bfloat16),
            jax.ShapeDtypeStruct((DIRECT, WIDTH), jnp.bfloat16),
            jax.ShapeDtypeStruct((2 * SPILL, WIDTH), jnp.bfloat16),
        ],
        scratch_shapes=[
            pltpu.VMEM(tokens.shape, tokens.dtype),
            pltpu.VMEM(grads.shape, grads.dtype),
            pltpu.SemaphoreType.DMA((2,)),
        ],
        compiler_params=pltpu.CompilerParams(vmem_limit_bytes=12 * MIB),
        cost_estimate=pl.CostEstimate(flops=10**9, bytes_accessed=4 * MIB, transcendentals=0),
        name="pack",
    )(me, routes, in_hbm(tokens), in_hbm(grads))


def choose_kernel(choice_ref, *refs):
    for k, ref in enumerate(refs[:-1]):
        refs[-1][k * SPILL : (k + 1) * SPILL, :] = ref[...]


def choose(choice, blocks):
    count = len(blocks)
    return pl.pallas_call(
        choose_kernel,
        grid_spec=pltpu.PrefetchScalarGridSpec(
            num_scalar_prefetch=1,
            grid=(1,),
            in_specs=[pl.BlockSpec((SPILL, WIDTH), lambda i, c: (c[SLOT_BESIDE], 0))] * count,
            out_specs=pl.BlockSpec((count * SPILL, WIDTH), lambda i, c: (0, 0)),
        ),
        out_shape=jax.ShapeDtypeStruct((count * SPILL, WIDTH), jnp.bfloat16),
        compiler_params=pltpu.CompilerParams(vmem_limit_bytes=4 * MIB),
        cost_estimate=pl.CostEstimate(
            flops=0, bytes_accessed=4 * count * SPILL * WIDTH, transcendentals=0
        ),
        name="choose",
    )(choice, *blocks)


def hop_kernel(choice_ref, *refs):
    for k in range(len(HOPS)):
        refs[len(HOPS) + k][...] = refs[k][...]


def hop_rows(choice, blocks):
    return pl.pallas_call(
        hop_kernel,
        grid_spec=pltpu.PrefetchScalarGridSpec(
            num_scalar_prefetch=1,
            grid=(1,),
            in_specs=[
                pl.BlockSpec((SPILL, WIDTH), lambda i, c, k=k: (c[SLOT_HOP + k], 0))
                for k in range(len(HOPS))
            ],
            out_specs=[pl.BlockSpec((SPILL, WIDTH), lambda i, c: (0, 0))] * len(HOPS),
        ),
        out_shape=[jax.ShapeDtypeStruct((SPILL, WIDTH), jnp.bfloat16)] * len(HOPS),
        compiler_params=pltpu.CompilerParams(vmem_limit_bytes=6 * MIB),
        cost_estimate=pl.CostEstimate(
            flops=0, bytes_accessed=4 * len(HOPS) * SPILL * WIDTH, transcendentals=0
        ),
        name="hop_rows",
    )(choice, *[blocks[from_above] for from_above, _, _ in HOPS])


def deltas(x, dh, wg, wu):
    gate = jnp.dot(x, wg, preferred_element_type=jnp.float32)
    up = jnp.dot(x, wu, preferred_element_type=jnp.float32)
    sig = jax.nn.sigmoid(gate)
    wide = dh.astype(jnp.float32)
    delta_g = (wide * up * sig * (1.0 + gate * (1.0 - sig))).astype(jnp.bfloat16)
    delta_u = (wide * gate * sig).astype(jnp.bfloat16)
    return delta_g, delta_u


def put_deltas(ref, j, delta_g, delta_u):
    for first, delta in ((0, delta_g), (FF, delta_u)):
        ref[:, pl.ds(pl.multiple_of(first + j * FF_BLOCK, FF_BLOCK), FF_BLOCK)] = delta


def back_rows(delta_g, delta_u, wg, wu):
    dims = (((1,), (1,)), ((), ()))
    return lax.dot_general(
        delta_g, wg, dims, preferred_element_type=jnp.float32
    ) + lax.dot_general(delta_u, wu, dims, preferred_element_type=jnp.float32)


def over_kernel(choice_ref, *refs):
    inputs = 5 + len(PIECES) + len(HOPS)
    wg_ref, wu_ref, x_ref, delta_ref, back_ref, acc_ref, dh_ref = refs[inputs:]
    j = pl.program_id(0)
    last = pl.num_programs(0) - 1
    hot = choice_ref[HOT_ME] == 1

    @pl.when(j == 0)
    def _():
        back_ref[...] = jnp.zeros_like(back_ref)
        at = 0
        for ref in refs[:inputs]:
            rows = ref.shape[0]
            x_ref[at : at + rows, :] = ref[:, :D]
            for k in range(FF // FF_BLOCK):
                dh_ref[k, at : at + rows, :] = ref[
                    :, D + k * FF_BLOCK : D + (k + 1) * FF_BLOCK
                ]
            at += rows

    @pl.when(jnp.logical_not(hot))
    def _():
        delta_ref[...] = jnp.zeros_like(delta_ref)

    @pl.when(hot)
    def _():
        delta_g, delta_u = deltas(x_ref[...], dh_ref[j], wg_ref[0], wu_ref[0])
        put_deltas(delta_ref, j, delta_g, delta_u)
        part = back_rows(delta_g, delta_u, wg_ref[0], wu_ref[0])

        @pl.when(j == 0)
        def _():
            acc_ref[...] = part

        @pl.when(jnp.logical_and(j > 0, j < last))
        def _():
            acc_ref[...] += part

        @pl.when(j == last)
        def _():
            acc_ref[...] += part
            me = choice_ref[ME]
            for k in range(2 * len(OFFSETS)):
                source = (me + 2 * OFFSETS[k % 8] + EXPERTS) % EXPERTS
                if k >= 8:
                    source = source + 1 - 2 * (source % 2)
                row = pl.multiple_of(source * CAP + COLD, COLD)
                back_ref[pl.ds(row, SPILL), :] = acc_ref[
                    k * SPILL : (k + 1) * SPILL, :
                ].astype(jnp.bfloat16)


def over(choice, column, rest, w_gate, w_up):
    steps = FF // FF_BLOCK

    def whole(a):
        return pl.BlockSpec(a.shape, lambda j, c: (0, 0))

    return pl.pallas_call(
        over_kernel,
        grid_spec=pltpu.PrefetchScalarGridSpec(
            num_scalar_prefetch=1,
            grid=(steps,),
            in_specs=[pl.BlockSpec((SPILL, WIDTH), lambda j, c: (c[SLOT_ME], 0))] * len(column)
            + [whole(a) for a in rest]
            + [pl.BlockSpec((1, D, FF_BLOCK), lambda j, c: (0, 0, j))] * 2,
            out_specs=[
                pl.BlockSpec((OVER, D), lambda j, c: (0, 0)),
                pl.BlockSpec((OVER, 2 * FF), lambda j, c: (0, 0)),
                pl.BlockSpec((ROWS, D), lambda j, c: (0, 0)),
            ],
            scratch_shapes=[
                pltpu.VMEM((OVER, D), jnp.float32),
                pltpu.VMEM((steps, OVER, FF_BLOCK), jnp.bfloat16),
            ],
        ),
        out_shape=[
            pltpu.HBM((OVER, D), jnp.bfloat16),
            pltpu.HBM((OVER, 2 * FF), jnp.bfloat16),
            pltpu.HBM((ROWS, D), jnp.bfloat16),
        ],
        compiler_params=pltpu.CompilerParams(vmem_limit_bytes=34 * MIB),
        cost_estimate=pl.CostEstimate(
            flops=8 * OVER * D * FF, bytes_accessed=17 * MIB, transcendentals=OVER * FF
        ),
        name="over",
    )(choice, *column, *rest, w_gate, w_up)


def direct_kernel(
    got_ref,
    all_wg_ref,
    all_wu_ref,
    old_ref,
    delta_ref,
    back_ref,
    wg_ref,
    wu_ref,
    low_ref,
    high_ref,
    in_sems,
    out_sems,
):
    parts = [slice(k * FF_BLOCK, (k + 1) * FF_BLOCK) for k in range(FF // FF_BLOCK)]
    loads = [
        [
            pltpu.make_async_copy(all_ref.at[0, :, part], ref.at[:, part], in_sems.at[which, k])
            for which, (all_ref, ref) in enumerate(((all_wg_ref, wg_ref), (all_wu_ref, wu_ref)))
        ]
        for k, part in enumerate(parts)
    ]
    for pair in loads:
        for load in pair:
            load.start()
    x = got_ref[:, :D]
    for k, part in enumerate(parts):
        for load in loads[k]:
            load.wait()
        dh = got_ref[:, D + part.start : D + part.stop]
        delta_g, delta_u = deltas(x, dh, wg_ref[:, part], wu_ref[:, part])
        delta_ref[:, part] = delta_g
        delta_ref[:, FF + part.start : FF + part.stop] = delta_u
    width = D // 4
    stores = []
    for q in range(4):
        rows = slice(q * width, (q + 1) * width)
        back = back_rows(delta_ref[:, :FF], delta_ref[:, FF:], wg_ref[rows, :], wu_ref[rows, :])
        half_ref = low_ref if q < 2 else high_ref
        half_ref[:, q % 2 * width : (q % 2 + 1) * width] = back.astype(jnp.bfloat16)
        if q % 2 == 1:
            columns = slice((q - 1) * width, (q + 1) * width)
            for e in range(EXPERTS):
                store = pltpu.make_async_copy(
                    half_ref.at[e * COLD : (e + 1) * COLD, :],
                    back_ref.at[e * CAP : e * CAP + COLD, columns],
                    out_sems.at[q // 2, e],
                )
                store.start()
                stores.append(store)
    for store in stores:
        store.wait()


def direct(got, w_gate, w_up, back):
    vmem = pl.BlockSpec(memory_space=pltpu.VMEM)
    hbm = pl.BlockSpec(memory_space=pltpu.HBM)
    return pl.pallas_call(
        direct_kernel,
        in_specs=[vmem, hbm, hbm, hbm],
        out_specs=[vmem, hbm],
        out_shape=[
            pltpu.HBM((DIRECT, 2 * FF), jnp.bfloat16),
            pltpu.HBM((ROWS, D), jnp.bfloat16),
        ],
        scratch_shapes=[
            pltpu.VMEM((D, FF), jnp.bfloat16),
            pltpu.VMEM((D, FF), jnp.bfloat16),
            pltpu.VMEM((DIRECT, D // 2), jnp.bfloat16),
            pltpu.VMEM((DIRECT, D // 2), jnp.bfloat16),
            pltpu.SemaphoreType.DMA((2, FF // FF_BLOCK)),
            pltpu.SemaphoreType.DMA((2, EXPERTS)),
        ],
        input_output_aliases={3: 1},
        compiler_params=pltpu.CompilerParams(vmem_limit_bytes=24 * MIB),
        cost_estimate=pl.CostEstimate(
            flops=8 * DIRECT * D * FF, bytes_accessed=10 * MIB, transcendentals=DIRECT * FF
        ),
        name="direct",
    )(got, w_gate, w_up, pltpu.with_memory_space_constraint(back, pltpu.HBM))


def turned(x_ref, turned_ref, block_ref, first):
    for q in range(turned_ref.shape[0] // BLOCK):
        column = pl.multiple_of(block_ref[first + q] * BLOCK, BLOCK)
        turned_ref[q * BLOCK : (q + 1) * BLOCK, :] = x_ref[:, pl.ds(column, BLOCK)].T


def weight_over_kernel(block_ref, choice_ref, x_ref, delta_ref, out_ref, turned_ref):
    hot = choice_ref[HOT_ME] == 1

    @pl.when(hot)
    def _():
        @pl.when(pl.program_id(0) == 0)
        def _():
            turned(x_ref, turned_ref, block_ref, 0)

        out_ref[...] = jnp.dot(
            turned_ref[...], delta_ref[...], preferred_element_type=jnp.float32
        )

    @pl.when(jnp.logical_not(hot))
    def _():
        out_ref[...] = jnp.zeros_like(out_ref)


def weight_over(blocks, choice, x, delta):
    rows = blocks.shape[0] * BLOCK
    return pl.pallas_call(
        weight_over_kernel,
        grid_spec=pltpu.PrefetchScalarGridSpec(
            num_scalar_prefetch=2,
            grid=(2 * FF // FF_BLOCK,),
            in_specs=[
                pl.BlockSpec((OVER, D), lambda j, b, c: (0, 0)),
                pl.BlockSpec((OVER, FF_BLOCK), lambda j, b, c: (0, j)),
            ],
            out_specs=pl.BlockSpec((rows, FF_BLOCK), lambda j, b, c: (0, j)),
            scratch_shapes=[pltpu.VMEM((rows, OVER), jnp.bfloat16)],
        ),
        out_shape=pltpu.HBM((rows, 2 * FF), jnp.float32),
        compiler_params=pltpu.CompilerParams(vmem_limit_bytes=20 * MIB),
        cost_estimate=pl.CostEstimate(
            flops=4 * OVER * rows * FF, bytes_accessed=17 * MIB, transcendentals=0
        ),
        name="weight_over",
    )(blocks, choice, x, delta)


def weight_send_kernel(block_ref, x_ref, delta_ref, part_ref, out_ref, turned_ref):
    @pl.when(pl.program_id(0) == 0)
    def _():
        turned(x_ref, turned_ref, block_ref, 0)

    total = part_ref[...] + jnp.dot(
        turned_ref[...], delta_ref[...], preferred_element_type=jnp.float32
    )
    out_ref[...] = total.astype(jnp.bfloat16)


def weight_specs(rows, half):
    return [
        pl.BlockSpec((DIRECT, D), lambda j, b: (0, 0)),
        pl.BlockSpec((DIRECT, FF_BLOCK), lambda j, b: (0, j)),
        pl.BlockSpec((rows, FF_BLOCK), lambda j, b: (half, j)),
    ]


def weight_send(blocks, arrays):
    rows = blocks.shape[0] // 2 * BLOCK
    return pl.pallas_call(
        weight_send_kernel,
        grid_spec=pltpu.PrefetchScalarGridSpec(
            num_scalar_prefetch=1,
            grid=(2 * FF // FF_BLOCK,),
            in_specs=weight_specs(rows, 0),
            out_specs=pl.BlockSpec((rows, FF_BLOCK), lambda j, b: (0, j)),
            scratch_shapes=[pltpu.VMEM((rows, DIRECT), jnp.bfloat16)],
        ),
        out_shape=jax.ShapeDtypeStruct((rows, 2 * FF), jnp.bfloat16),
        compiler_params=pltpu.CompilerParams(vmem_limit_bytes=14 * MIB),
        cost_estimate=pl.CostEstimate(
            flops=4 * DIRECT * rows * FF, bytes_accessed=11 * MIB, transcendentals=0
        ),
        name="weight_send",
    )(blocks, *arrays)


def weight_keep_kernel(block_ref, x_ref, delta_ref, part_ref, came_ref, *refs):
    *out_refs, turned_ref = refs

    @pl.when(pl.program_id(0) == 0)
    def _():
        turned(x_ref, turned_ref, block_ref, block_ref.shape[0] // 2)

    total = jnp.dot(turned_ref[...], delta_ref[...], preferred_element_type=jnp.float32)
    total = total + part_ref[...] + came_ref[...].astype(jnp.float32)
    for k, out_ref in enumerate(out_refs):
        rows = out_ref.shape[0]
        out_ref[...] = total[k * rows : (k + 1) * rows, :].astype(out_ref.dtype)


def weight_keep(blocks, arrays, came):
    rows = blocks.shape[0] // 2 * BLOCK
    count = rows // BLOCK
    return pl.pallas_call(
        weight_keep_kernel,
        grid_spec=pltpu.PrefetchScalarGridSpec(
            num_scalar_prefetch=1,
            grid=(2 * FF // FF_BLOCK,),
            in_specs=weight_specs(rows, 1) + [pl.BlockSpec((rows, FF_BLOCK), lambda j, b: (0, j))],
            out_specs=[pl.BlockSpec((BLOCK, FF_BLOCK), lambda j, b: (0, j))] * count,
            scratch_shapes=[pltpu.VMEM((rows, DIRECT), jnp.bfloat16)],
        ),
        out_shape=[jax.ShapeDtypeStruct((BLOCK, 2 * FF), jnp.float32)] * 2
        + [jax.ShapeDtypeStruct((BLOCK, 2 * FF), jnp.bfloat16)] * (count - 2),
        compiler_params=pltpu.CompilerParams(vmem_limit_bytes=16 * MIB),
        cost_estimate=pl.CostEstimate(
            flops=4 * DIRECT * rows * FF, bytes_accessed=14 * MIB, transcendentals=0
        ),
        name="weight_keep",
    )(blocks, *arrays, came)


def place(index):
    return index // 4, index // 2 % 2, index % 2


def partner(index, step):
    y, x, core = place(index)
    return (y + step // 2) % 4 * 4 + (x + step % 2) % 2 * 2 + core


def per_device(tokens, routes, grad_hidden, w_gate, w_up):
    groups = lax.axis_size("dp")
    steps = groups // 2
    expert_at = lax.axis_index("expert")
    choice, sel, send, spill = pack(
        expert_at.reshape(1).astype(jnp.int32),
        routes.T,
        tokens,
        grad_hidden.transpose(1, 0, 2),
    )
    choice = choice.reshape(128)
    w_gate, w_up = in_hbm(w_gate), in_hbm(w_up)
    ups = [(e, (e + 2) % EXPERTS) for e in range(EXPERTS)]
    downs = [(e, (e - 2) % EXPERTS) for e in range(EXPERTS)]
    beside = [(e, e ^ 1) for e in range(EXPERTS)]

    column = [spill]
    right = left = spill
    for _ in range(2):
        right = lax.ppermute(right, "expert", ups)
        left = lax.ppermute(left, "expert", downs)
        column += [right, left]
    hops = [
        lax.ppermute(
            block, "expert", [(e, target(e, step, crosses)) for e in range(EXPERTS)]
        )
        for block, (_, step, crosses) in zip(hop_rows(choice, (right, left)), HOPS)
    ]
    pieces = [lax.ppermute(choose(choice, column[a:b]), "expert", beside) for a, b in PIECES]
    crossing = [hop for hop, (_, _, crosses) in zip(hops, HOPS) if crosses]
    rest = [hop for hop, (_, _, crosses) in zip(hops, HOPS) if not crosses] + pieces + crossing
    send, *rest = lax.optimization_barrier((send, *rest))
    got = lax.all_to_all(send, "expert", split_axis=0, concat_axis=0, tiled=True)
    rest = [in_hbm(a) for a in rest]
    over_x, over_delta, back = over(choice, column, rest, w_gate, w_up)
    keep = [[partner(i, s) for s in range(steps)] for i in range(groups)]
    table = np.array([[b ^ 1 for b in row] + row for row in keep], np.int32)
    blocks = jnp.asarray(table)[lax.axis_index("dp")]
    part = weight_over(blocks, choice, in_hbm(over_x), in_hbm(over_delta))
    got, part = lax.optimization_barrier((got, part))
    delta, back = direct(got, w_gate, w_up, back)
    returned = lax.all_to_all(back, "expert", split_axis=0, concat_axis=0, tiled=True)
    rows = (got, in_hbm(delta), in_hbm(part))
    other_half = weight_send(blocks, rows)
    came = lax.ppermute(other_half, "dp", [(i, i ^ 1) for i in range(groups)])
    halves = weight_keep(blocks, rows, came)
    sums = list(halves[:2])
    for half in (1, 0):
        for s in (4, 2, 6):
            came = lax.ppermute(
                halves[s + half], "dp", [(i, partner(i, s)) for i in range(groups)]
            )
            sums[half] = sums[half] + came.astype(jnp.float32)
        if half == 1:
            across = lax.ppermute(
                sums[1].astype(jnp.bfloat16), "dp", [(i, partner(i, 1)) for i in range(groups)]
            )
    grad_tokens = jnp.dot(sel, returned, preferred_element_type=jnp.float32).astype(jnp.bfloat16)
    across, grad_tokens = lax.optimization_barrier((across, grad_tokens))
    total = sums[0] + across.astype(jnp.float32)
    return grad_tokens, total[None, :, :FF], total[None, :, FF:]


def solution(mesh):
    placed = (
        P(("dp", "expert"), None),
        P(("dp", "expert"), None),
        P(("dp", "expert"), None, None),
        P("expert", None, None),
        P("expert", None, None),
    )
    return jax.shard_map(
        per_device,
        mesh=mesh,
        in_specs=placed,
        out_specs=(P(("dp", "expert"), None), P("expert", "dp", None), P("expert", "dp", None)),
        check_vma=False,
    )
```

```python
import functools

import jax
import jax.numpy as jnp
import numpy as np
from jax import lax
from jax.experimental import pallas as pl
from jax.experimental.pallas import tpu as pltpu
from jax.sharding import PartitionSpec as P

D = 2048
FF = 768
EXPERTS = 16
COLD = 16
SPILL = 32
CAP = COLD + SPILL
ROWS = EXPERTS * CAP
DIRECT = EXPERTS * COLD
OVER = EXPERTS * SPILL
WIDTH = D + FF
OFFSETS = (0, -1, 1, -2, 2, 4, -3, 3)
PIECES = ((0, 5),)
SLOT_ME, HOT_ME, SLOT_BESIDE, ME = range(4)
HOPS = ((0, 2, False), (1, -2, True), (0, 1, False), (1, -1, False), (0, 1, True), (1, -1, True))
SLOT_HOP = 4
BLOCK = 128
FF_BLOCK = 256
MIB = 1 << 20


def target(expert, step, crosses):
    there = (expert + 2 * step + EXPERTS) % EXPERTS
    return there + 1 - 2 * (there % 2) if crosses else there


def in_hbm(a):
    return pltpu.with_memory_space_constraint(a, pltpu.HBM)


def pack_kernel(
    me_ref,
    routes_ref,
    all_tokens_ref,
    all_grads_ref,
    choice_ref,
    sel_ref,
    out_ref,
    over_ref,
    tokens_ref,
    grads_ref,
    sems,
):
    copies = [
        pltpu.make_async_copy(all_tokens_ref, tokens_ref, sems.at[0]),
        pltpu.make_async_copy(all_grads_ref, grads_ref, sems.at[1]),
    ]
    for copy in copies:
        copy.start()
    toks = routes_ref.shape[1]
    me = me_ref[0]
    routes = [routes_ref[k : k + 1, :] for k in range(2)]
    expert_ids = lax.broadcasted_iota(jnp.int32, (EXPERTS, toks), 0)
    members = [(r == expert_ids).astype(jnp.float32) for r in routes]
    member = members[0] + members[1]
    member_low = member.astype(jnp.bfloat16)
    token_down = lax.broadcasted_iota(jnp.int32, (toks, toks), 0)
    token_across = lax.broadcasted_iota(jnp.int32, (toks, toks), 1)
    before = jnp.dot(
        member_low,
        (token_down < token_across).astype(jnp.bfloat16),
        preferred_element_type=jnp.float32,
    )

    def of_pair(table):
        return [jnp.sum(m * table, axis=0, keepdims=True).astype(jnp.int32) for m in members]

    ranks = of_pair(before)

    count_col = jnp.sum(member, axis=1, keepdims=True)
    count_row = lax.dot_general(
        jnp.ones((8, toks), jnp.bfloat16),
        member_low,
        (((1,), (1,)), ((), ())),
        preferred_element_type=jnp.float32,
    )[:1]
    down = lax.broadcasted_iota(jnp.int32, (EXPERTS, EXPERTS), 0)
    across = lax.broadcasted_iota(jnp.int32, (EXPERTS, EXPERTS), 1)
    above_col = jnp.sum((count_row > count_col).astype(jnp.float32), axis=1, keepdims=True)
    above_row = jnp.sum((count_col > count_row).astype(jnp.float32), axis=0, keepdims=True)
    hot_col = (above_col < 1.5).astype(jnp.float32)
    hot_row = (above_row < 1.5).astype(jnp.float32)
    which_col = jnp.sum(hot_row * (across < down).astype(jnp.float32), axis=1, keepdims=True)
    which_row = jnp.sum(hot_col * (down < across).astype(jnp.float32), axis=0, keepdims=True)
    whiches = of_pair(which_col)

    lane16 = lax.broadcasted_iota(jnp.int32, (1, EXPERTS), 1)

    def at_expert(expert, row):
        return jnp.sum(
            jnp.where(lane16 == expert, row, 0.0), axis=1, keepdims=True
        ).astype(jnp.int32)

    slots = hot_row * which_row
    values = {
        SLOT_ME: at_expert(me, slots),
        HOT_ME: at_expert(me, hot_row),
        SLOT_BESIDE: at_expert(target(me, 0, True), slots),
        ME: me,
    }
    for k, (_, step, crosses) in enumerate(HOPS):
        values[SLOT_HOP + k] = at_expert(target(me, step, crosses), slots)
    lane = lax.broadcasted_iota(jnp.int32, (1, 128), 1)
    choice = jnp.zeros((1, 128), jnp.int32)
    for at, value in values.items():
        choice = jnp.where(lane == at, value, choice)
    choice_ref[...] = choice

    def picked(slots, rows):
        at = lax.broadcasted_iota(jnp.int32, (rows, toks), 0)
        return [(slot == at).astype(jnp.bfloat16) for slot in slots]

    def fill(ref, slots):
        first, second = picked(slots, ref.shape[0])
        ref[:, :D] = jnp.dot(
            first + second, tokens_ref[...], preferred_element_type=jnp.float32
        ).astype(jnp.bfloat16)
        ref[:, D:] = (
            jnp.dot(first, grads_ref[0], preferred_element_type=jnp.float32)
            + jnp.dot(second, grads_ref[1], preferred_element_type=jnp.float32)
        ).astype(jnp.bfloat16)

    first, second = picked([r * CAP + rank for r, rank in zip(routes, ranks)], ROWS)
    sel_ref[...] = lax.dot_general(
        (token_down == token_across).astype(jnp.bfloat16),
        first + second,
        (((1,), (1,)), ((), ())),
        preferred_element_type=jnp.float32,
    ).astype(jnp.bfloat16)
    for copy in copies:
        copy.wait()
    fill(
        over_ref,
        [
            jnp.where(rank >= COLD, which * SPILL + rank - COLD, -1)
            for which, rank in zip(whiches, ranks)
        ],
    )
    fill(
        out_ref,
        [jnp.where(rank < COLD, r * COLD + rank, -1) for r, rank in zip(routes, ranks)],
    )


def pack(me, routes, tokens, grads):
    toks = tokens.shape[0]
    vmem = pl.BlockSpec(memory_space=pltpu.VMEM)
    hbm = pl.BlockSpec(memory_space=pltpu.HBM)
    return pl.pallas_call(
        pack_kernel,
        in_specs=[pl.BlockSpec(memory_space=pltpu.SMEM), vmem, hbm, hbm],
        out_specs=[vmem] * 4,
        out_shape=[
            jax.ShapeDtypeStruct((1, 128), jnp.int32),
            pltpu.HBM((toks, ROWS), jnp.bfloat16),
            jax.ShapeDtypeStruct((DIRECT, WIDTH), jnp.bfloat16),
            jax.ShapeDtypeStruct((2 * SPILL, WIDTH), jnp.bfloat16),
        ],
        scratch_shapes=[
            pltpu.VMEM(tokens.shape, tokens.dtype),
            pltpu.VMEM(grads.shape, grads.dtype),
            pltpu.SemaphoreType.DMA((2,)),
        ],
        compiler_params=pltpu.CompilerParams(vmem_limit_bytes=12 * MIB),
        cost_estimate=pl.CostEstimate(flops=10**9, bytes_accessed=4 * MIB, transcendentals=0),
        name="pack",
    )(me, routes, in_hbm(tokens), in_hbm(grads))


def choose_kernel(choice_ref, *refs):
    for k, ref in enumerate(refs[:-1]):
        refs[-1][k * SPILL : (k + 1) * SPILL, :] = ref[...]


def choose(choice, blocks):
    count = len(blocks)
    return pl.pallas_call(
        choose_kernel,
        grid_spec=pltpu.PrefetchScalarGridSpec(
            num_scalar_prefetch=1,
            grid=(1,),
            in_specs=[pl.BlockSpec((SPILL, WIDTH), lambda i, c: (c[SLOT_BESIDE], 0))] * count,
            out_specs=pl.BlockSpec((count * SPILL, WIDTH), lambda i, c: (0, 0)),
        ),
        out_shape=jax.ShapeDtypeStruct((count * SPILL, WIDTH), jnp.bfloat16),
        compiler_params=pltpu.CompilerParams(vmem_limit_bytes=8 * MIB),
        cost_estimate=pl.CostEstimate(
            flops=0, bytes_accessed=4 * count * SPILL * WIDTH, transcendentals=0
        ),
        name="choose",
    )(choice, *blocks)


def hop_kernel(choice_ref, *refs):
    for k in range(len(HOPS)):
        refs[len(HOPS) + k][...] = refs[k][...]


def hop_rows(choice, blocks):
    return pl.pallas_call(
        hop_kernel,
        grid_spec=pltpu.PrefetchScalarGridSpec(
            num_scalar_prefetch=1,
            grid=(1,),
            in_specs=[
                pl.BlockSpec((SPILL, WIDTH), lambda i, c, k=k: (c[SLOT_HOP + k], 0))
                for k in range(len(HOPS))
            ],
            out_specs=[pl.BlockSpec((SPILL, WIDTH), lambda i, c: (0, 0))] * len(HOPS),
        ),
        out_shape=[jax.ShapeDtypeStruct((SPILL, WIDTH), jnp.bfloat16)] * len(HOPS),
        compiler_params=pltpu.CompilerParams(vmem_limit_bytes=6 * MIB),
        cost_estimate=pl.CostEstimate(
            flops=0, bytes_accessed=4 * len(HOPS) * SPILL * WIDTH, transcendentals=0
        ),
        name="hop_rows",
    )(choice, *[blocks[from_above] for from_above, _, _ in HOPS])


def deltas(x, dh, wg, wu):
    gate = jnp.dot(x, wg, preferred_element_type=jnp.float32)
    up = jnp.dot(x, wu, preferred_element_type=jnp.float32)
    sig = jax.nn.sigmoid(gate)
    wide = dh.astype(jnp.float32)
    delta_g = (wide * up * sig * (1.0 + gate * (1.0 - sig))).astype(jnp.bfloat16)
    delta_u = (wide * gate * sig).astype(jnp.bfloat16)
    return delta_g, delta_u


def put_deltas(ref, j, delta_g, delta_u):
    for first, delta in ((0, delta_g), (FF, delta_u)):
        ref[:, pl.ds(pl.multiple_of(first + j * FF_BLOCK, FF_BLOCK), FF_BLOCK)] = delta


def back_rows(delta_g, delta_u, wg, wu):
    dims = (((1,), (1,)), ((), ()))
    return lax.dot_general(
        delta_g, wg, dims, preferred_element_type=jnp.float32
    ) + lax.dot_general(delta_u, wu, dims, preferred_element_type=jnp.float32)


def over_kernel(choice_ref, *refs):
    inputs = 5 + len(PIECES) + len(HOPS)
    wg_ref, wu_ref, x_ref, delta_ref, back_ref, acc_ref, dh_ref = refs[inputs:]
    j = pl.program_id(0)
    last = pl.num_programs(0) - 1
    hot = choice_ref[HOT_ME] == 1

    @pl.when(j == 0)
    def _():
        back_ref[...] = jnp.zeros_like(back_ref)
        at = 0
        for ref in refs[:inputs]:
            rows = ref.shape[0]
            x_ref[at : at + rows, :] = ref[:, :D]
            for k in range(FF // FF_BLOCK):
                dh_ref[k, at : at + rows, :] = ref[
                    :, D + k * FF_BLOCK : D + (k + 1) * FF_BLOCK
                ]
            at += rows

    @pl.when(jnp.logical_not(hot))
    def _():
        delta_ref[...] = jnp.zeros_like(delta_ref)

    @pl.when(hot)
    def _():
        delta_g, delta_u = deltas(x_ref[...], dh_ref[j], wg_ref[0], wu_ref[0])
        put_deltas(delta_ref, j, delta_g, delta_u)
        part = back_rows(delta_g, delta_u, wg_ref[0], wu_ref[0])

        @pl.when(j == 0)
        def _():
            acc_ref[...] = part

        @pl.when(jnp.logical_and(j > 0, j < last))
        def _():
            acc_ref[...] += part

        @pl.when(j == last)
        def _():
            acc_ref[...] += part
            me = choice_ref[ME]
            for k in range(2 * len(OFFSETS)):
                source = (me + 2 * OFFSETS[k % 8] + EXPERTS) % EXPERTS
                if k >= 8:
                    source = source + 1 - 2 * (source % 2)
                row = pl.multiple_of(source * CAP + COLD, COLD)
                back_ref[pl.ds(row, SPILL), :] = acc_ref[
                    k * SPILL : (k + 1) * SPILL, :
                ].astype(jnp.bfloat16)


def over(choice, column, rest, w_gate, w_up):
    steps = FF // FF_BLOCK

    def whole(a):
        return pl.BlockSpec(a.shape, lambda j, c: (0, 0))

    return pl.pallas_call(
        over_kernel,
        grid_spec=pltpu.PrefetchScalarGridSpec(
            num_scalar_prefetch=1,
            grid=(steps,),
            in_specs=[pl.BlockSpec((SPILL, WIDTH), lambda j, c: (c[SLOT_ME], 0))] * len(column)
            + [whole(a) for a in rest]
            + [pl.BlockSpec((1, D, FF_BLOCK), lambda j, c: (0, 0, j))] * 2,
            out_specs=[
                pl.BlockSpec((OVER, D), lambda j, c: (0, 0)),
                pl.BlockSpec((OVER, 2 * FF), lambda j, c: (0, 0)),
                pl.BlockSpec((ROWS, D), lambda j, c: (0, 0)),
            ],
            scratch_shapes=[
                pltpu.VMEM((OVER, D), jnp.float32),
                pltpu.VMEM((steps, OVER, FF_BLOCK), jnp.bfloat16),
            ],
        ),
        out_shape=[
            pltpu.HBM((OVER, D), jnp.bfloat16),
            pltpu.HBM((OVER, 2 * FF), jnp.bfloat16),
            pltpu.HBM((ROWS, D), jnp.bfloat16),
        ],
        compiler_params=pltpu.CompilerParams(vmem_limit_bytes=34 * MIB),
        cost_estimate=pl.CostEstimate(
            flops=8 * OVER * D * FF, bytes_accessed=17 * MIB, transcendentals=OVER * FF
        ),
        name="over",
    )(choice, *column, *rest, w_gate, w_up)


def direct_kernel(
    got_ref,
    all_wg_ref,
    all_wu_ref,
    old_ref,
    delta_ref,
    back_ref,
    wg_ref,
    wu_ref,
    low_ref,
    high_ref,
    in_sems,
    out_sems,
):
    parts = [slice(k * FF_BLOCK, (k + 1) * FF_BLOCK) for k in range(FF // FF_BLOCK)]
    loads = [
        [
            pltpu.make_async_copy(all_ref.at[0, :, part], ref.at[:, part], in_sems.at[which, k])
            for which, (all_ref, ref) in enumerate(((all_wg_ref, wg_ref), (all_wu_ref, wu_ref)))
        ]
        for k, part in enumerate(parts)
    ]
    for pair in loads:
        for load in pair:
            load.start()
    x = got_ref[:, :D]
    for k, part in enumerate(parts):
        for load in loads[k]:
            load.wait()
        dh = got_ref[:, D + part.start : D + part.stop]
        delta_g, delta_u = deltas(x, dh, wg_ref[:, part], wu_ref[:, part])
        delta_ref[:, part] = delta_g
        delta_ref[:, FF + part.start : FF + part.stop] = delta_u
    width = D // 4
    stores = []
    for q in range(4):
        rows = slice(q * width, (q + 1) * width)
        back = back_rows(delta_ref[:, :FF], delta_ref[:, FF:], wg_ref[rows, :], wu_ref[rows, :])
        half_ref = low_ref if q < 2 else high_ref
        half_ref[:, q % 2 * width : (q % 2 + 1) * width] = back.astype(jnp.bfloat16)
        if q % 2 == 1:
            columns = slice((q - 1) * width, (q + 1) * width)
            for e in range(EXPERTS):
                store = pltpu.make_async_copy(
                    half_ref.at[e * COLD : (e + 1) * COLD, :],
                    back_ref.at[e * CAP : e * CAP + COLD, columns],
                    out_sems.at[q // 2, e],
                )
                store.start()
                stores.append(store)
    for store in stores:
        store.wait()


def direct(got, w_gate, w_up, back):
    vmem = pl.BlockSpec(memory_space=pltpu.VMEM)
    hbm = pl.BlockSpec(memory_space=pltpu.HBM)
    return pl.pallas_call(
        direct_kernel,
        in_specs=[vmem, hbm, hbm, hbm],
        out_specs=[vmem, hbm],
        out_shape=[
            pltpu.HBM((DIRECT, 2 * FF), jnp.bfloat16),
            pltpu.HBM((ROWS, D), jnp.bfloat16),
        ],
        scratch_shapes=[
            pltpu.VMEM((D, FF), jnp.bfloat16),
            pltpu.VMEM((D, FF), jnp.bfloat16),
            pltpu.VMEM((DIRECT, D // 2), jnp.bfloat16),
            pltpu.VMEM((DIRECT, D // 2), jnp.bfloat16),
            pltpu.SemaphoreType.DMA((2, FF // FF_BLOCK)),
            pltpu.SemaphoreType.DMA((2, EXPERTS)),
        ],
        input_output_aliases={3: 1},
        compiler_params=pltpu.CompilerParams(vmem_limit_bytes=24 * MIB),
        cost_estimate=pl.CostEstimate(
            flops=8 * DIRECT * D * FF, bytes_accessed=10 * MIB, transcendentals=DIRECT * FF
        ),
        name="direct",
    )(got, w_gate, w_up, pltpu.with_memory_space_constraint(back, pltpu.HBM))


def turned(x_ref, turned_ref, block_ref, first):
    for q in range(turned_ref.shape[0] // BLOCK):
        column = pl.multiple_of(block_ref[first + q] * BLOCK, BLOCK)
        turned_ref[q * BLOCK : (q + 1) * BLOCK, :] = x_ref[:, pl.ds(column, BLOCK)].T


def weight_over_kernel(block_ref, choice_ref, x_ref, delta_ref, out_ref, turned_ref):
    hot = choice_ref[HOT_ME] == 1

    @pl.when(hot)
    def _():
        @pl.when(pl.program_id(0) == 0)
        def _():
            turned(x_ref, turned_ref, block_ref, 0)

        out_ref[...] = jnp.dot(
            turned_ref[...], delta_ref[...], preferred_element_type=jnp.float32
        )

    @pl.when(jnp.logical_not(hot))
    def _():
        out_ref[...] = jnp.zeros_like(out_ref)


def weight_over(blocks, choice, x, delta):
    rows = blocks.shape[0] * BLOCK
    return pl.pallas_call(
        weight_over_kernel,
        grid_spec=pltpu.PrefetchScalarGridSpec(
            num_scalar_prefetch=2,
            grid=(2 * FF // FF_BLOCK,),
            in_specs=[
                pl.BlockSpec((OVER, D), lambda j, b, c: (0, 0)),
                pl.BlockSpec((OVER, FF_BLOCK), lambda j, b, c: (0, j)),
            ],
            out_specs=pl.BlockSpec((rows, FF_BLOCK), lambda j, b, c: (0, j)),
            scratch_shapes=[pltpu.VMEM((rows, OVER), jnp.bfloat16)],
        ),
        out_shape=pltpu.HBM((rows, 2 * FF), jnp.float32),
        compiler_params=pltpu.CompilerParams(vmem_limit_bytes=20 * MIB),
        cost_estimate=pl.CostEstimate(
            flops=4 * OVER * rows * FF, bytes_accessed=17 * MIB, transcendentals=0
        ),
        name="weight_over",
    )(blocks, choice, x, delta)


def weight_send_kernel(block_ref, x_ref, delta_ref, part_ref, out_ref, turned_ref):
    @pl.when(pl.program_id(0) == 0)
    def _():
        turned(x_ref, turned_ref, block_ref, 0)

    total = part_ref[...] + jnp.dot(
        turned_ref[...], delta_ref[...], preferred_element_type=jnp.float32
    )
    out_ref[...] = total.astype(jnp.bfloat16)


def weight_specs(rows, half):
    return [
        pl.BlockSpec((DIRECT, D), lambda j, b: (0, 0)),
        pl.BlockSpec((DIRECT, FF_BLOCK), lambda j, b: (0, j)),
        pl.BlockSpec((rows, FF_BLOCK), lambda j, b: (half, j)),
    ]


def weight_send(blocks, arrays):
    rows = blocks.shape[0] // 2 * BLOCK
    return pl.pallas_call(
        weight_send_kernel,
        grid_spec=pltpu.PrefetchScalarGridSpec(
            num_scalar_prefetch=1,
            grid=(2 * FF // FF_BLOCK,),
            in_specs=weight_specs(rows, 0),
            out_specs=pl.BlockSpec((rows, FF_BLOCK), lambda j, b: (0, j)),
            scratch_shapes=[pltpu.VMEM((rows, DIRECT), jnp.bfloat16)],
        ),
        out_shape=jax.ShapeDtypeStruct((rows, 2 * FF), jnp.bfloat16),
        compiler_params=pltpu.CompilerParams(vmem_limit_bytes=14 * MIB),
        cost_estimate=pl.CostEstimate(
            flops=4 * DIRECT * rows * FF, bytes_accessed=11 * MIB, transcendentals=0
        ),
        name="weight_send",
    )(blocks, *arrays)


def weight_keep_kernel(block_ref, x_ref, delta_ref, part_ref, came_ref, *refs):
    *out_refs, turned_ref = refs

    @pl.when(pl.program_id(0) == 0)
    def _():
        turned(x_ref, turned_ref, block_ref, block_ref.shape[0] // 2)

    total = jnp.dot(turned_ref[...], delta_ref[...], preferred_element_type=jnp.float32)
    total = total + part_ref[...] + came_ref[...].astype(jnp.float32)
    for k, out_ref in enumerate(out_refs):
        rows = out_ref.shape[0]
        out_ref[...] = total[k * rows : (k + 1) * rows, :].astype(out_ref.dtype)


def weight_keep(blocks, arrays, came):
    rows = blocks.shape[0] // 2 * BLOCK
    count = rows // BLOCK
    return pl.pallas_call(
        weight_keep_kernel,
        grid_spec=pltpu.PrefetchScalarGridSpec(
            num_scalar_prefetch=1,
            grid=(2 * FF // FF_BLOCK,),
            in_specs=weight_specs(rows, 1) + [pl.BlockSpec((rows, FF_BLOCK), lambda j, b: (0, j))],
            out_specs=[pl.BlockSpec((BLOCK, FF_BLOCK), lambda j, b: (0, j))] * count,
            scratch_shapes=[pltpu.VMEM((rows, DIRECT), jnp.bfloat16)],
        ),
        out_shape=[jax.ShapeDtypeStruct((BLOCK, 2 * FF), jnp.float32)] * 2
        + [jax.ShapeDtypeStruct((BLOCK, 2 * FF), jnp.bfloat16)] * (count - 2),
        compiler_params=pltpu.CompilerParams(vmem_limit_bytes=16 * MIB),
        cost_estimate=pl.CostEstimate(
            flops=4 * DIRECT * rows * FF, bytes_accessed=14 * MIB, transcendentals=0
        ),
        name="weight_keep",
    )(blocks, *arrays, came)


def place(index):
    return index // 4, index // 2 % 2, index % 2


def partner(index, step):
    y, x, core = place(index)
    return (y + step // 2) % 4 * 4 + (x + step % 2) % 2 * 2 + core


def per_device(tokens, routes, grad_hidden, w_gate, w_up):
    groups = lax.axis_size("dp")
    steps = groups // 2
    expert_at = lax.axis_index("expert")
    choice, sel, send, spill = pack(
        expert_at.reshape(1).astype(jnp.int32),
        routes.T,
        tokens,
        grad_hidden.transpose(1, 0, 2),
    )
    choice = choice.reshape(128)
    w_gate, w_up = in_hbm(w_gate), in_hbm(w_up)
    ups = [(e, (e + 2) % EXPERTS) for e in range(EXPERTS)]
    downs = [(e, (e - 2) % EXPERTS) for e in range(EXPERTS)]
    beside = [(e, e ^ 1) for e in range(EXPERTS)]

    column = [spill]
    right = left = spill
    for _ in range(2):
        right = lax.ppermute(right, "expert", ups)
        left = lax.ppermute(left, "expert", downs)
        column += [right, left]
    hops = [
        lax.ppermute(
            block, "expert", [(e, target(e, step, crosses)) for e in range(EXPERTS)]
        )
        for block, (_, step, crosses) in zip(hop_rows(choice, (right, left)), HOPS)
    ]
    pieces = [lax.ppermute(choose(choice, column[a:b]), "expert", beside) for a, b in PIECES]
    crossing = [hop for hop, (_, _, crosses) in zip(hops, HOPS) if crosses]
    rest = [hop for hop, (_, _, crosses) in zip(hops, HOPS) if not crosses] + pieces + crossing
    send, *rest = lax.optimization_barrier((send, *rest))
    got = lax.all_to_all(send, "expert", split_axis=0, concat_axis=0, tiled=True)
    rest = [in_hbm(a) for a in rest]
    over_x, over_delta, back = over(choice, column, rest, w_gate, w_up)
    keep = [[partner(i, s) for s in range(steps)] for i in range(groups)]
    table = np.array([[b ^ 1 for b in row] + row for row in keep], np.int32)
    blocks = jnp.asarray(table)[lax.axis_index("dp")]
    part = weight_over(blocks, choice, in_hbm(over_x), in_hbm(over_delta))
    got, part = lax.optimization_barrier((got, part))
    delta, back = direct(got, w_gate, w_up, back)
    returned = lax.all_to_all(back, "expert", split_axis=0, concat_axis=0, tiled=True)
    rows = (got, in_hbm(delta), in_hbm(part))
    other_half = weight_send(blocks, rows)
    came = lax.ppermute(other_half, "dp", [(i, i ^ 1) for i in range(groups)])
    halves = weight_keep(blocks, rows, came)
    sums = list(halves[:2])
    for half in (1, 0):
        for s in (4, 2, 6):
            came = lax.ppermute(
                halves[s + half], "dp", [(i, partner(i, s)) for i in range(groups)]
            )
            sums[half] = sums[half] + came.astype(jnp.float32)
        if half == 1:
            across = lax.ppermute(
                sums[1].astype(jnp.bfloat16), "dp", [(i, partner(i, 1)) for i in range(groups)]
            )
    grad_tokens = jnp.dot(sel, returned, preferred_element_type=jnp.float32).astype(jnp.bfloat16)
    across, grad_tokens = lax.optimization_barrier((across, grad_tokens))
    total = sums[0] + across.astype(jnp.float32)
    return grad_tokens, total[None, :, :FF], total[None, :, FF:]


def solution(mesh):
    placed = (
        P(("dp", "expert"), None),
        P(("dp", "expert"), None),
        P(("dp", "expert"), None, None),
        P("expert", None, None),
        P("expert", None, None),
    )
    return jax.shard_map(
        per_device,
        mesh=mesh,
        in_specs=placed,
        out_specs=(P(("dp", "expert"), None), P("expert", "dp", None), P("expert", "dp", None)),
        check_vma=False,
    )
```
